512 devices in a mesh: st: 8 (over x, core), fsdp: 64 (over z, y).
Axes of the slice: x: 4, y: 8, z: 8, core: 2. Of those that a mesh axis runs over, the one named last changes fastest.
Arguments:
- normed: bfloat16 [64, 512, 3072], P('fsdp')
- qkv_weight: bfloat16 [3072, 32, 384], P('fsdp', 'st'), may hold values from -0.109375 to 0.109375
- out_weight: bfloat16 [3072, 4096], P('fsdp', 'st'), may hold values from -0.09375 to 0.09375
- segment_ids: int32 [64], replicated, may hold values from 0 to 15, never falling along the last dimension, each value on 1 to 8 neighbouring positions
Outputs:
- attended: bfloat16 [64, 512, 3072], P('fsdp', 'st')
The draws below stay inside these ranges and needn't reach their ends.
Inputs may be any that keep to these rules, and one draw needn't show every extreme that they name: `segment_ids`: segment ids never fall from one frame to the next; each clip covers 1 to 8 consecutive frames, and one covers exactly 8.
All inputs are finite; a program needn't handle non-finite values.
Results may differ from the reference program's by a relative error of at most 0.017.
Values may be sent and summed in bfloat16 or wider, within the bound.
A program may use at most 64 MiB of HBM per device.

```python
import math
import jax
import jax.numpy as jnp
import numpy as np
from jax import lax

D = 3072
HEAD = 128
HS_DEV = 2
HT_DEV = 2
P_SIZE = 512
CLIP = 8
HEADS = 32
FRAMES = 64
SEGS = 16
N_ST = 8


def draw_normed(key, part):
    first = jax.random.fold_in(key, 0)
    return jax.random.normal(first, (FRAMES, P_SIZE, D), jnp.float32).astype(jnp.bfloat16)


def block_scale(stream_key, dims, pieces, least, top_value):
    loudness = 1.0
    for axis_at, parts in pieces:
        draws = jax.random.uniform(jax.random.fold_in(jax.random.fold_in(stream_key, 6), axis_at), (parts,), jnp.float32, least / len(pieces), top_value / len(pieces))
        loudness = loudness * jnp.repeat(jnp.exp(draws), dims[axis_at] // parts).reshape((-1,) + (1,) * (len(dims) - 1 - axis_at))
    return loudness


def profile(amount, total, bound, lean):
    loads = [(1 << 20) // math.isqrt(standing ** lean) + 1 for standing in range(2, amount + 1)]
    rest, counts = total - bound - (amount - 1), [1] * (amount - 1)
    while rest > 0:
        movable = [i for i in range(amount - 1) if counts[i] < bound]
        mass, left = sum([loads[i] for i in movable]), rest
        for i in movable:
            addition = min(bound - counts[i], max(1, left * loads[i] // mass), rest)
            counts[i] = counts[i] + addition
            rest = rest - addition
    return np.array([bound] + counts)


def uneven(key, count, total, reach, skew):
    if count == 2:
        one = jax.random.randint(key, (), max(1, total - reach), min(reach, total - 1) + 1)
        return jnp.stack([one, total - one])
    sizes = jnp.asarray(profile(count, total, reach, skew), jnp.int32)
    couples = (count - 1) // 2
    giver, sink = sizes[1:1 + 2 * couples:2], sizes[2:2 + 2 * couples:2]
    margin = jnp.minimum(giver - 1, reach - sink)
    moved = jax.random.randint(jax.random.fold_in(key, 1), (couples,), 0, 1 << 20) % (margin + 1)
    sizes = sizes.at[1:1 + 2 * couples:2].set(giver - moved).at[2:2 + 2 * couples:2].set(sink + moved)
    return sizes[jax.random.permutation(jax.random.fold_in(key, 2), count)]


def normal_values(rng, dims, scale, most, cuts=(), kind=jnp.bfloat16):
    loudness = block_scale(rng, dims, cuts, -0.22, 0.18) if cuts else 1.0
    array = jax.random.normal(rng, dims, jnp.float32) * scale * loudness
    return jnp.minimum(jnp.maximum(array, -most), most).astype(kind)


def setup_inputs(seed: int = 0) -> dict:
    seeds = jax.random.split(jax.random.key(seed), 5)
    normed = draw_normed(jax.random.fold_in(seeds[4], 71), 0)
    qkv_weight = normal_values(seeds[1], (D, HEADS, 3 * HEAD), D ** -0.5, 0.109375, ((0, 64), (1, 8)))
    out_weight = normal_values(seeds[2], (D, HEADS * HEAD), (HEADS * HEAD) ** -0.5, 0.09375, ((0, 64), (1, 8)))
    segment_ids = jnp.searchsorted(jnp.cumsum(uneven(seeds[3], SEGS, FRAMES, CLIP, 0)), jnp.arange(FRAMES), side="right").astype(jnp.int32)
    return dict(normed=normed, qkv_weight=qkv_weight, out_weight=out_weight, segment_ids=segment_ids)


def softmax_rows(scores):
    top = lax.optimization_barrier(jnp.max(scores, axis=-1, keepdims=True))
    expo = jnp.exp(scores - top)
    return expo / lax.optimization_barrier(jnp.sum(expo, axis=-1, keepdims=True))

def reference(normed, qkv_weight, out_weight, segment_ids):
    group = HS_DEV + HT_DEV
    scale = 1.0 / math.sqrt(HEAD)
    weight_flat = qkv_weight.reshape(D, HEADS * 3 * HEAD)

    def frame_work(frame):
        packed = jnp.dot(frame, weight_flat, preferred_element_type=jnp.float32).astype(jnp.bfloat16)
        packed = packed.reshape(P_SIZE, N_ST, group, 3 * HEAD)
        spatial = packed[:, :, :HS_DEV].reshape(P_SIZE, N_ST * HS_DEV, 3 * HEAD).astype(jnp.float32)
        query = spatial[..., :HEAD]
        keys = spatial[..., HEAD:2 * HEAD]
        values = spatial[..., 2 * HEAD:]
        scores = jnp.einsum('qhc,khc->hqk', query, keys) * scale
        weights = softmax_rows(scores).astype(jnp.bfloat16).astype(jnp.float32)
        spatial_out = jnp.einsum('hqk,khc->qhc', weights, values).astype(jnp.bfloat16)
        return (spatial_out.reshape(P_SIZE, N_ST, HS_DEV, HEAD), packed[:, :, HS_DEV:])
    spatial_out, temporal = lax.map(frame_work, normed)
    temporal = temporal.astype(jnp.float32)
    query = temporal[..., :HEAD]
    keys = temporal[..., HEAD:2 * HEAD]
    values = temporal[..., 2 * HEAD:]
    scores = jnp.einsum('tpshc,upshc->pshtu', query, keys) * scale
    same = segment_ids[:, None] == segment_ids[None, :]
    scores = jnp.where(same, scores, jnp.float32(-1e+30))
    weights = softmax_rows(scores).astype(jnp.bfloat16).astype(jnp.float32)
    temporal_out = jnp.einsum('pshtu,upshc->tpshc', weights, values).astype(jnp.bfloat16)
    heads_out = jnp.concatenate([spatial_out, temporal_out], axis=3)
    heads_out = heads_out.reshape(FRAMES * P_SIZE, N_ST, group * HEAD)
    out_groups = out_weight.reshape(D, N_ST, group * HEAD)
    total = jnp.zeros((FRAMES * P_SIZE, D), jnp.float32)
    for index in range(N_ST):
        partial_sum = lax.dot_general(heads_out[:, index], out_groups[:, index], (((1,), (1,)), ((), ())), preferred_element_type=jnp.float32)
        total = total + partial_sum.astype(jnp.bfloat16).astype(jnp.float32)
    return total.astype(jnp.bfloat16).reshape(FRAMES, P_SIZE, D)
```

```python
import functools
import math

import jax
import jax.numpy as jnp
from jax import lax
from jax.experimental import pallas as pl
from jax.experimental.pallas import tpu as pltpu
from jax.sharding import PartitionSpec as P

HEAD = 128
MESH = pl.DeviceIdType.MESH
NZ = NY = 8
NX = 4
PIECE = 48
QKV = 3 * HEAD
SLAB = 384
PATCHES = 512
WIDTH = 3072
UP = ((-1, 0), (-1, 1), (-2, 0), (-2, 1), (-3, 0), (-3, 1), (-4, 0))
DOWN = ((1, 1), (1, 0), (2, 1), (2, 0), (3, 1), (3, 0), (4, 1))
F32 = jnp.float32
BF16 = jnp.bfloat16


def nt_dot(a, b):
    return lax.dot_general(a, b, (((1,), (1,)), ((), ())), preferred_element_type=F32)


def nn_dot(a, b):
    return lax.dot_general(a, b, (((1,), (0,)), ((), ())), preferred_element_type=F32)


def softmax_rows(scores):
    top = jnp.max(scores, axis=-1, keepdims=True)
    expo = jnp.exp(scores - top)
    return expo * (1.0 / jnp.sum(expo, axis=-1, keepdims=True))


def kernel(
    seg_ref, x_ref, x4_ref, wq_ref, wo_ref, out_ref,
    xs, w, wo, r1, a, xt, acc, qt, qs, ot, b1, b2, ho, p, c, d, f, idc, idr,
    gs, gr, ns, nr, hs, hr, ts, tr, vs, vr, loc,
):
    st, fs = lax.axis_index("st"), lax.axis_index("fsdp")
    x, core = st // 2, st % 2
    z, y = fs // NY, fs % NY
    scale = 1.0 / math.sqrt(HEAD)
    sent = []

    def dev_y(k):
        return (st, z * NY + (y + k) % NY)

    def dev_z(k):
        return (st, ((z + k) % NZ) * NY + y)

    def dev_x(k):
        return (((x + k) % NX) * 2 + core, fs)

    sibling = (x * 2 + 1 - core, fs)

    def remote(src, dst, ssem, rsem, dev):
        return pltpu.make_async_remote_copy(
            src_ref=src, dst_ref=dst, send_sem=ssem, recv_sem=rsem, device_id=dev, device_id_type=MESH
        )

    def send(*args):
        copy = remote(*args)
        copy.start()
        sent.append(copy)

    barrier = pltpu.get_barrier_semaphore()
    for k in range(1, 8):
        pl.semaphore_signal(barrier, inc=1, device_id=dev_y(k), device_id_type=MESH)
        pl.semaphore_signal(barrier, inc=1, device_id=dev_z(k), device_id_type=MESH)
    for k in range(1, 4):
        pl.semaphore_signal(barrier, inc=1, device_id=dev_x(k), device_id_type=MESH)
    pl.semaphore_signal(barrier, inc=1, device_id=sibling, device_id_type=MESH)
    pl.semaphore_wait(barrier, 18)

    class Stream:
        def __init__(self, number, y_first, flip, own, view):
            self.n, self.y_first, self.flip, self.own, self.view = number, y_first, flip, own, view
            self.ac, self.bc = (y, z) if y_first else (z, y)
            self.da, self.db = (dev_y, dev_z) if y_first else (dev_z, dev_y)

        def piece(self, at):
            return self.view(self.bc, at) if self.y_first else self.view(at, self.bc)

        def slab(self, bt, sub):
            four = pl.ds(4 * sub, 4)
            return self.view(bt, four) if self.y_first else self.view(four, bt)

        def sems(self, i):
            return gs.at[self.n, i], gr.at[self.n, i]

        def first_own(self):
            right = 1 if not self.flip else -1
            send(self.own, self.piece(self.ac), *self.sems(0), self.da(right))
            send(self.own, self.piece(self.ac), *self.sems(4), self.da(-right))

        def first(self, k):
            right = 1 if not self.flip else -1
            for way, base, last in ((right, 0, 4), (-right, 4, 3)):
                if k <= last:
                    got = self.piece((self.ac - way * k) % 8)
                    remote(got, got, *self.sems(base + k - 1), self.da(-way)).wait_recv()
                    if k < last:
                        send(got, got, *self.sems(base + k), self.da(way))

        def second_own(self):
            for sub in (0, 1):
                for way, base, chain in ((1, 7, UP), (-1, 14, DOWN)):
                    blk = self.slab(self.bc, chain[sub][1])
                    send(blk, blk, *self.sems(base + sub), self.db(way))

        def second(self, i):
            for way, base, chain in ((1, 7, UP), (-1, 14, DOWN)):
                off, sub = chain[i]
                got = self.slab((self.bc + off) % 8, sub)
                remote(got, got, *self.sems(base + i), self.db(-way)).wait_recv()
                if i <= 4:
                    send(got, got, *self.sems(base + i + 2), self.db(way))

    def head_stream(number, h, y_first, flip):
        return Stream(number, y_first, flip, wq_ref.at[h], lambda zi, yi: w.at[h, zi, yi])

    s0 = head_stream(2, 0, True, True)
    s1 = head_stream(3, 1, False, True)
    t0 = head_stream(0, 2, True, False)
    t1 = head_stream(1, 3, False, False)
    o0 = Stream(4, True, False, wo_ref.at[pl.ds(0, 32)], lambda zi, yi: wo.at[zi, yi, pl.ds(0, 32)])
    o1 = Stream(5, False, False, wo_ref.at[pl.ds(32, 16)], lambda zi, yi: wo.at[zi, yi, pl.ds(32, 16)])

    cols = pl.ds(pl.multiple_of(st * SLAB, SLAB), SLAB)
    for k in range(1, 8):
        yy = (y + k) % NY
        send(x4_ref.at[:, yy, :, cols], r1.at[y], ns.at[k - 1], nr.at[k - 1], dev_y(k))
    for s in (t0, t1, s0, s1, o1, o0):
        s.first_own()
    locals_ = [
        pltpu.make_async_copy(x4_ref.at[:, y, :, cols], r1.at[y], loc.at[0]),
        pltpu.make_async_copy(wo_ref, wo.at[z, y], loc.at[1]),
    ]
    for h in range(4):
        locals_.append(pltpu.make_async_copy(wq_ref.at[h], w.at[h, z, y], loc.at[2 + h]))
    locals_.append(pltpu.make_async_copy(x_ref, xs, loc.at[6]))
    for cp in locals_:
        cp.start()

    sub8 = lax.broadcasted_iota(jnp.int32, (8, HEAD), 0)
    lane = lax.broadcasted_iota(jnp.int32, (8, PATCHES), 1)
    row = jnp.zeros((8, PATCHES), jnp.int32)
    for t in range(64):
        sid = seg_ref[t]
        idc[t * 8 : (t + 1) * 8, :] = sub8 + sid * 8
        row = jnp.where(lane // 8 == t, sid * 8, row)
    idr[...] = row + lane % 8

    for cp in locals_[:6]:
        cp.wait()

    for k in range(1, 5):
        t0.first(k)
        t1.first(k)
    t0.second_own()
    t1.second_own()
    for k in range(1, 8):
        got = r1.at[(y - k) % NY]
        remote(got, got, ns.at[k - 1], nr.at[k - 1], dev_y(-k)).wait_recv()
    for k in range(1, 8):
        zz = (z + k) % NZ
        send(r1.at[:, zz], a.at[st, z], ns.at[6 + k], nr.at[6 + k], dev_z(k))
    own_tile = pltpu.make_async_copy(r1.at[:, z], a.at[st, z], loc.at[7])
    own_tile.start()
    for k in range(1, 5):
        for s in (s0, s1, o1, o0):
            s.first(k)
    own_tile.wait()
    t0.second(0)
    t1.second(0)
    for k in range(1, 8):
        got = a.at[st, (z - k) % NZ]
        remote(got, got, ns.at[6 + k], nr.at[6 + k], dev_z(-k)).wait_recv()
    sl_m, sl_p, sl_2 = (((x + k) % NX) * 2 + core for k in (3, 1, 2))
    send(a.at[st], a.at[st], ns.at[14], nr.at[14], dev_x(1))
    send(a.at[st], a.at[st], ns.at[15], nr.at[15], dev_x(-1))
    send(a.at[st], a.at[st], ns.at[18], nr.at[18], sibling)
    t0.second(1)
    t1.second(1)

    def assemble(sl):
        def body(i, _):
            v = a[sl, i].astype(F32).reshape(64, SLAB)
            xt[sl, pl.ds(pl.multiple_of(i * 64, 64), 64), :] = v.astype(BF16)
            return 0

        lax.fori_loop(0, 8, body, 0)

    assemble(st)
    t0.second(2)
    t1.second(2)
    lo, hi = pl.ds(0, 4), pl.ds(4, 4)
    remote(a.at[sl_m], a.at[sl_m], ns.at[14], nr.at[14], dev_x(-1)).wait_recv()
    send(a.at[sl_m, lo], a.at[sl_m, lo], ns.at[16], nr.at[16], dev_x(1))
    send(a.at[sl_m], a.at[sl_m], ns.at[19], nr.at[19], sibling)
    remote(a.at[sl_p], a.at[sl_p], ns.at[15], nr.at[15], dev_x(1)).wait_recv()
    send(a.at[sl_p, hi], a.at[sl_p, hi], ns.at[17], nr.at[17], dev_x(-1))
    send(a.at[sl_p], a.at[sl_p], ns.at[20], nr.at[20], sibling)
    assemble(sl_m)
    assemble(sl_p)
    t0.second(3)
    t1.second(3)
    remote(a.at[sl_2, lo], a.at[sl_2, lo], ns.at[16], nr.at[16], dev_x(-1)).wait_recv()
    remote(a.at[sl_2, hi], a.at[sl_2, hi], ns.at[17], nr.at[17], dev_x(1)).wait_recv()
    send(a.at[sl_2], a.at[sl_2], ns.at[21], nr.at[21], sibling)
    assemble(sl_2)
    t0.second(4)
    t1.second(4)
    s0.second_own()
    s1.second_own()
    flip = 1 - 2 * core
    for i, sl in enumerate((st, sl_m, sl_p, sl_2)):
        other = sl + flip
        remote(a.at[other], a.at[other], ns.at[18 + i], nr.at[18 + i], sibling).wait_recv()
        assemble(other)
    for i in (5, 6):
        t0.second(i)
        t1.second(i)

    def proj(load, h, dest):
        acc[...] = jnp.zeros_like(acc)

        def body(i, _):
            acc[...] += nn_dot(load(i), w[h, i].reshape(SLAB, QKV))
            return 0

        lax.fori_loop(0, 8, body, 0)
        dest[...] = acc[...].astype(BF16)

    proj(lambda i: xt[i], 2, qt.at[0])
    s0.second(0)
    s1.second(0)
    proj(lambda i: xt[i], 3, qt.at[1])
    s0.second(1)
    s1.second(1)

    for h in (0, 1):
        for b, start in enumerate((0, 64, 192, 256)):
            rows, keys = pl.ds(b * 128, 128), pl.ds(start, 256)
            s = nt_dot(qt[h, rows, 0:HEAD], qt[h, keys, HEAD : 2 * HEAD]) * scale
            same = idc[rows, 0:1] == idr[0:1, keys]
            wt = softmax_rows(jnp.where(same, s, -1e30)).astype(BF16)
            o = nn_dot(wt, qt[h, keys, 2 * HEAD :])
            ot[2 * b : 2 * b + 2, :, :, h * HEAD : (h + 1) * HEAD] = o.reshape(2, 8, 8, HEAD).astype(BF16)
    for k in range(1, 8):
        zz = (z + k) % NZ
        send(ot.at[zz], b1.at[z], ts.at[k - 1], tr.at[k - 1], dev_z(k))
    back = pltpu.make_async_copy(ot.at[z], b1.at[z], loc.at[8])
    back.start()
    s0.second(2)
    s1.second(2)
    back.wait()
    for k in range(1, 8):
        got = b1.at[(z - k) % NZ]
        remote(got, got, ts.at[k - 1], tr.at[k - 1], dev_z(-k)).wait_recv()
    for k in range(1, 8):
        yy = (y + k) % NY
        send(b1.at[:, yy], b2.at[:, y], ts.at[6 + k], tr.at[6 + k], dev_y(k))
    back2 = pltpu.make_async_copy(b1.at[:, y], b2.at[:, y], loc.at[9])
    back2.start()
    s0.second(3)
    s1.second(3)
    s0.second(4)
    s1.second(4)
    o1.second_own()
    o0.second_own()
    for i in (5, 6):
        s0.second(i)
        s1.second(i)
    locals_[6].wait()
    back2.wait()

    def own_rows(i):
        return xs[:, pl.ds(pl.multiple_of(i * SLAB, SLAB), SLAB)]

    def spatial(h):
        def body(i, _):
            rows = pl.ds(pl.multiple_of(i * 128, 128), 128)
            s = nt_dot(qs[h, rows, 0:HEAD], qs[h, :, HEAD : 2 * HEAD]) * scale
            o = nn_dot(softmax_rows(s).astype(BF16), qs[h, :, 2 * HEAD :])
            ho[rows, h * HEAD : (h + 1) * HEAD] = o.astype(BF16)
            return 0

        lax.fori_loop(0, 4, body, 0)

    proj(own_rows, 0, qs.at[0])
    o1.second(0)
    o0.second(0)
    proj(own_rows, 1, qs.at[1])
    o1.second(1)
    o0.second(1)
    spatial(0)
    o1.second(2)
    o0.second(2)
    spatial(1)
    o1.second(3)
    o0.second(3)
    for k in range(1, 8):
        got = b2.at[:, (y - k) % NY]
        remote(got, got, ts.at[6 + k], tr.at[6 + k], dev_y(-k)).wait_recv()
    for i in range(8):
        ho[i * 64 : (i + 1) * 64, 2 * HEAD :] = b2[i].astype(F32).reshape(64, 2 * HEAD).astype(BF16)
    for i in (4, 5, 6):
        o1.second(i)

    order = (0, -1, 1, -2, 2, -3, 3, 4)

    def project(j):
        n = (z + order[j]) % NZ
        o = nt_dot(ho[...], wo[n].reshape(SLAB, 4 * HEAD))
        p[j] = o.astype(BF16).reshape(NX, 2, 64, SLAB)
        send(p.at[j, :, 1 - core], c.at[j], vs.at[j, 0], vr.at[j, 0], sibling)

    def pair(j):
        remote(c.at[j], c.at[j], vs.at[j, 0], vr.at[j, 0], sibling).wait_recv()
        d[j] = (p[j, :, core].astype(F32) + c[j].astype(F32)).astype(BF16)
        for k in (1, 2, 3):
            send(d.at[j, (x + k) % NX], f.at[j, k - 1], vs.at[j, k], vr.at[j, k], dev_x(k))

    def finish(j):
        total = d[j, x].astype(F32)
        for k in (1, 2, 3):
            got = f.at[j, k - 1]
            remote(got, got, vs.at[j, k], vr.at[j, k], dev_x(-k)).wait_recv()
            total = total + f[j, k - 1].astype(F32)
        n = (z + order[j]) % NZ
        out_ref[:, pl.ds(pl.multiple_of(n * SLAB, SLAB), SLAB)] = total.astype(BF16)

    for j in range(5):
        project(j)
        if j >= 1:
            pair(j - 1)
    o0.second(4)
    o0.second(5)
    project(5)
    pair(4)
    project(6)
    pair(5)
    o0.second(6)
    project(7)
    pair(6)
    pair(7)
    for j in range(8):
        finish(j)
    for copy in sent:
        copy.wait_send()


def shards(normed, qkv_weight, out_weight, segment_ids):
    rows = normed.reshape(PATCHES, WIDTH)
    tiles = normed.reshape(NZ, NY, 8, WIDTH)
    heads = jnp.transpose(qkv_weight, (1, 0, 2))
    dma = pltpu.SemaphoreType.DMA
    out = pl.pallas_call(
        kernel,
        out_shape=jax.ShapeDtypeStruct((64, WIDTH), BF16),
        in_specs=[pl.BlockSpec(memory_space=pltpu.SMEM)] + [pl.BlockSpec(memory_space=pl.ANY)] * 4,
        out_specs=pl.BlockSpec(memory_space=pltpu.VMEM),
        scratch_shapes=[
            pltpu.VMEM((PATCHES, WIDTH), BF16),
            pltpu.VMEM((4, NZ, NY, PIECE, QKV), BF16),
            pltpu.VMEM((NZ, NY, PIECE, 4 * HEAD), BF16),
            pltpu.VMEM((NY, NZ, 8, SLAB), BF16),
            pltpu.VMEM((8, NZ, NY, 8, SLAB), BF16),
            pltpu.VMEM((8, PATCHES, SLAB), BF16),
            pltpu.VMEM((PATCHES, QKV), F32),
            pltpu.VMEM((2, PATCHES, QKV), BF16),
            pltpu.VMEM((2, PATCHES, QKV), BF16),
            pltpu.VMEM((NZ, NY, 8, 2 * HEAD), BF16),
            pltpu.VMEM((NZ, NY, 8, 2 * HEAD), BF16),
            pltpu.VMEM((NZ, NY, 8, 2 * HEAD), BF16),
            pltpu.VMEM((PATCHES, 4 * HEAD), BF16),
            pltpu.VMEM((8, NX, 2, 64, SLAB), BF16),
            pltpu.VMEM((8, NX, 64, SLAB), BF16),
            pltpu.VMEM((8, NX, 64, SLAB), BF16),
            pltpu.VMEM((8, 3, 64, SLAB), BF16),
            pltpu.VMEM((PATCHES, HEAD), jnp.int32),
            pltpu.VMEM((8, PATCHES), jnp.int32),
            dma((6, 21)), dma((6, 21)),
            dma((22,)), dma((22,)),
            dma((1,)), dma((1,)),
            dma((14,)), dma((14,)),
            dma((8, 4)), dma((8, 4)),
            dma((10,)),
        ],
        compiler_params=pltpu.CompilerParams(
            collective_id=0, has_side_effects=True, vmem_limit_bytes=58 * 2**20
        ),
        name="whole",
    )(segment_ids, rows, tiles, heads, out_weight)
    return out.reshape(1, 64, WIDTH)


def solution(mesh):
    return jax.shard_map(
        shards,
        mesh=mesh,
        in_specs=(P("fsdp", None, None), P("fsdp", "st", None), P("fsdp", "st"), P()),
        out_specs=P("fsdp", "st", None),
        check_vma=False,
    )
```

```python
import functools
import math

import jax
import jax.numpy as jnp
from jax import lax
from jax.experimental import pallas as pl
from jax.experimental.pallas import tpu as pltpu
from jax.sharding import PartitionSpec as P

HEAD = 128
MESH = pl.DeviceIdType.MESH
NZ = NY = 8
NX = 4
PIECE = 48
QKV = 3 * HEAD
SLAB = 384
PATCHES = 512
WIDTH = 3072
UP = ((-1, 0), (-1, 1), (-2, 0), (-2, 1), (-3, 0), (-3, 1), (-4, 0))
DOWN = ((1, 1), (1, 0), (2, 1), (2, 0), (3, 1), (3, 0), (4, 1))
F32 = jnp.float32
BF16 = jnp.bfloat16


def nt_dot(a, b):
    return lax.dot_general(a, b, (((1,), (1,)), ((), ())), preferred_element_type=F32)


def nn_dot(a, b):
    return lax.dot_general(a, b, (((1,), (0,)), ((), ())), preferred_element_type=F32)


def softmax_rows(scores):
    top = jnp.max(scores, axis=-1, keepdims=True)
    expo = jnp.exp(scores - top)
    return expo * (1.0 / jnp.sum(expo, axis=-1, keepdims=True))


def kernel(
    seg_ref, x_ref, x4_ref, wq_ref, wo_ref, out_ref,
    xs, xt, w, wo, stage, a, acc, qt, qs, ot, b1, b2, ho, p, c, d, e, f, idc, idr,
    gs, gr, ns, nr, xsem, xrec, ts, tr, vs, vr, loc,
):
    st, fs = lax.axis_index("st"), lax.axis_index("fsdp")
    x, core = st // 2, st % 2
    z, y = fs // NY, fs % NY
    scale = 1.0 / math.sqrt(HEAD)
    sent = []

    def dev_y(k):
        return (st, z * NY + (y + k) % NY)

    def dev_z(k):
        return (st, ((z + k) % NZ) * NY + y)

    def dev_x(k):
        return (((x + k) % NX) * 2 + core, fs)

    sibling = (x * 2 + 1 - core, fs)

    def remote(src, dst, ssem, rsem, dev):
        return pltpu.make_async_remote_copy(
            src_ref=src, dst_ref=dst, send_sem=ssem, recv_sem=rsem, device_id=dev, device_id_type=MESH
        )

    def send(*args):
        copy = remote(*args)
        copy.start()
        sent.append(copy)

    barrier = pltpu.get_barrier_semaphore()

    def greet(k, _):
        pl.semaphore_signal(barrier, inc=1, device_id=(st, (fs + k) % 64), device_id_type=MESH)
        return 0

    lax.fori_loop(1, 64, greet, 0)
    for dev in (dev_x(1), dev_x(-1), sibling):
        pl.semaphore_signal(barrier, inc=1, device_id=dev, device_id_type=MESH)

    cols = pl.ds(pl.multiple_of(st * SLAB, SLAB), SLAB)
    locals_ = [
        pltpu.make_async_copy(x4_ref.at[:, :, :, cols], stage, loc.at[0]),
        pltpu.make_async_copy(wo_ref, wo.at[z, y], loc.at[1]),
        pltpu.make_async_copy(wq_ref.at[0], w.at[0, z, y], loc.at[2]),
        pltpu.make_async_copy(wq_ref.at[1], w.at[1, z, y], loc.at[3]),
        pltpu.make_async_copy(x_ref, xs, loc.at[4]),
    ]
    for cp in locals_:
        cp.start()

    sub8 = lax.broadcasted_iota(jnp.int32, (8, HEAD), 0)
    lane = lax.broadcasted_iota(jnp.int32, (8, PATCHES), 1)
    row = jnp.zeros((8, PATCHES), jnp.int32)
    for t in range(64):
        sid = seg_ref[t]
        idc[t * 8 : (t + 1) * 8, :] = sub8 + sid * 8
        row = jnp.where(lane // 8 == t, sid * 8, row)
    idr[...] = row + lane % 8

    for cp in locals_[:4]:
        cp.wait()
    own_tile = pltpu.make_async_copy(stage.at[z, y], a.at[st, z, y], loc.at[5])
    own_tile.start()
    own_tile.wait()
    pl.semaphore_wait(barrier, 66)

    class Stream:
        def __init__(self, number, y_first, flip, view):
            self.n, self.y_first, self.flip, self.view = number, y_first, flip, view
            self.ac, self.bc = (y, z) if y_first else (z, y)
            self.da, self.db = (dev_y, dev_z) if y_first else (dev_z, dev_y)

        def piece(self, at):
            return self.view(self.bc, at) if self.y_first else self.view(at, self.bc)

        def slab(self, bt, sub):
            four = pl.ds(4 * sub, 4)
            return self.view(bt, four) if self.y_first else self.view(four, bt)

        def sems(self, i):
            return gs.at[self.n, i], gr.at[self.n, i]

        def first_own(self):
            right = 1 if not self.flip else -1
            own = self.piece(self.ac)
            send(own, own, *self.sems(0), self.da(right))
            send(own, own, *self.sems(4), self.da(-right))

        def first(self, k):
            right = 1 if not self.flip else -1
            for way, base, last in ((right, 0, 4), (-right, 4, 3)):
                if k <= last:
                    got = self.piece((self.ac - way * k) % 8)
                    remote(got, got, *self.sems(base + k - 1), self.da(-way)).wait_recv()
                    if k < last:
                        send(got, got, *self.sems(base + k), self.da(way))

        def second_own(self):
            for sub in (0, 1):
                for way, base, chain in ((1, 7, UP), (-1, 14, DOWN)):
                    blk = self.slab(self.bc, chain[sub][1])
                    send(blk, blk, *self.sems(base + sub), self.db(way))

        def second(self, i):
            for way, base, chain in ((1, 7, UP), (-1, 14, DOWN)):
                off, sub = chain[i]
                got = self.slab((self.bc + off) % 8, sub)
                remote(got, got, *self.sems(base + i), self.db(-way)).wait_recv()
                if i <= 4:
                    send(got, got, *self.sems(base + i + 2), self.db(way))

    def head_stream(number, kind, h, y_first, flip):
        return Stream(number, y_first, flip, lambda zi, yi: w.at[kind, zi, yi, ..., pl.ds(h * QKV, QKV)])

    t0 = head_stream(0, 1, 0, True, False)
    t1 = head_stream(1, 1, 1, False, True)
    s0 = head_stream(2, 0, 0, True, True)
    s1 = head_stream(3, 0, 1, False, False)
    o0 = Stream(4, True, False, lambda zi, yi: wo.at[zi, yi, ..., pl.ds(0, 32), :])
    o1 = Stream(5, False, True, lambda zi, yi: wo.at[zi, yi, ..., pl.ds(32, 16), :])

    def both(one, two, i):
        one.second(i)
        two.second(i)

    t0.first_own()
    t1.first_own()

    def tile_out(k):
        to = (fs + k) % 64
        return remote(stage.at[to // NY, to % NY], a.at[st, z, y], ns.at[k - 1], nr.at[k - 1], (st, to))

    def tile_in(k):
        to = (fs + 64 - k) % 64
        got = a.at[st, to // NY, to % NY]
        return remote(got, got, ns.at[k - 1], nr.at[k - 1], (st, to))

    def start_tile(k, _):
        tile_out(k).start()
        return 0

    def await_tile(k, _):
        tile_in(k).wait_recv()
        return 0

    def end_tile(k, _):
        tile_out(k).wait_send()
        return 0

    lax.fori_loop(1, 64, start_tile, 0)
    others = (s0, s1, o1, o0)
    for s in others:
        s.first_own()
    for k in range(1, 5):
        t0.first(k)
        t1.first(k)
    t0.second_own()
    t1.second_own()

    def first_others(k):
        for s in others:
            s.first(k)

    def assemble(sl):
        def body(i, _):
            v = a[sl, i].astype(F32).reshape(64, SLAB).astype(BF16)
            rows = pl.ds(pl.multiple_of(i * 64, 64), 64)
            xt[rows, pl.ds(pl.multiple_of(sl * SLAB, SLAB), SLAB)] = v
            return 0

        lax.fori_loop(0, 8, body, 0)

    sl_m, sl_p, sl_2 = (((x + k) % NX) * 2 + core for k in (3, 1, 2))
    lo, hi = pl.ds(0, 4), pl.ds(4, 4)

    def xmove(ref, i, dev):
        return ref, ref, xsem.at[i], xrec.at[i], dev

    def from_sibling(i, sl):
        other = sl + 1 - 2 * core
        remote(*xmove(a.at[other], 4 + i, sibling)).wait_recv()
        assemble(other)

    first_others(1)
    first_others(2)
    both(t0, t1, 0)
    first_others(3)
    lax.fori_loop(1, 64, await_tile, 0)
    send(*xmove(a.at[st], 0, dev_x(1)))
    send(*xmove(a.at[st], 1, dev_x(-1)))
    send(*xmove(a.at[st], 4, sibling))
    both(t0, t1, 1)
    first_others(4)
    assemble(st)
    both(t0, t1, 2)
    remote(*xmove(a.at[sl_m], 0, dev_x(-1))).wait_recv()
    send(*xmove(a.at[sl_m, lo], 2, dev_x(1)))
    send(*xmove(a.at[sl_m], 5, sibling))
    remote(*xmove(a.at[sl_p], 1, dev_x(1))).wait_recv()
    send(*xmove(a.at[sl_p, hi], 3, dev_x(-1)))
    send(*xmove(a.at[sl_p], 6, sibling))
    assemble(sl_m)
    both(t0, t1, 3)
    assemble(sl_p)
    from_sibling(0, st)
    both(t0, t1, 4)
    s0.second_own()
    s1.second_own()
    remote(*xmove(a.at[sl_2, lo], 2, dev_x(-1))).wait_recv()
    remote(*xmove(a.at[sl_2, hi], 3, dev_x(1))).wait_recv()
    send(*xmove(a.at[sl_2], 7, sibling))
    assemble(sl_2)
    from_sibling(1, sl_m)
    both(t0, t1, 5)
    from_sibling(2, sl_p)
    from_sibling(3, sl_2)
    both(t0, t1, 6)

    def proj(rows, kind, i):
        part = nn_dot(rows[:, i * 2 * SLAB : (i + 1) * 2 * SLAB], w[kind, 2 * i : 2 * i + 2].reshape(2 * SLAB, 2 * QKV))
        acc[...] = part if i == 0 else acc[...] + part

    def temporal(h):
        base = h * QKV
        for b, start in enumerate((0, 64, 192, 256)):
            rows, keys = pl.ds(b * 128, 128), pl.ds(start, 256)
            s = nt_dot(qt[rows, base : base + HEAD], qt[keys, base + HEAD : base + 2 * HEAD]) * scale
            same = idc[rows, 0:1] == idr[0:1, keys]
            wt = softmax_rows(jnp.where(same, s, -1e30)).astype(BF16)
            o = nn_dot(wt, qt[keys, base + 2 * HEAD : base + QKV])
            ot[2 * b : 2 * b + 2, :, :, h * HEAD : (h + 1) * HEAD] = o.reshape(2, 8, 8, HEAD).astype(BF16)

    def spatial(h, half):
        base = h * QKV

        def body(i, _):
            rows = pl.ds(pl.multiple_of(i * 128, 128), 128)
            s = nt_dot(qs[rows, base : base + HEAD], qs[:, base + HEAD : base + 2 * HEAD]) * scale
            o = nn_dot(softmax_rows(s).astype(BF16), qs[:, base + 2 * HEAD : base + QKV])
            ho[rows, h * HEAD : (h + 1) * HEAD] = o.astype(BF16)
            return 0

        lax.fori_loop(2 * half, 2 * half + 2, body, 0)

    proj(xt, 1, 0)
    proj(xt, 1, 1)
    both(s0, s1, 0)
    proj(xt, 1, 2)
    proj(xt, 1, 3)
    qt[...] = acc[...].astype(BF16)
    both(s0, s1, 1)
    temporal(0)
    temporal(1)
    for k in range(1, 8):
        send(ot.at[(z + k) % NZ], b1.at[z], ts.at[k - 1], tr.at[k - 1], dev_z(k))
    back = pltpu.make_async_copy(ot.at[z], b1.at[z], loc.at[6])
    back.start()
    both(s0, s1, 2)
    back.wait()
    for k in range(1, 8):
        got = b1.at[(z - k) % NZ]
        remote(got, got, ts.at[k - 1], tr.at[k - 1], dev_z(-k)).wait_recv()
    for k in range(1, 8):
        send(b1.at[:, (y + k) % NY], b2.at[:, y], ts.at[6 + k], tr.at[6 + k], dev_y(k))
    back2 = pltpu.make_async_copy(b1.at[:, y], b2.at[:, y], loc.at[7])
    back2.start()
    both(s0, s1, 3)
    both(s0, s1, 4)
    o1.second_own()
    o0.second_own()
    both(s0, s1, 5)
    back2.wait()
    for k in range(1, 8):
        got = b2.at[:, (y - k) % NY]
        remote(got, got, ts.at[6 + k], tr.at[6 + k], dev_y(-k)).wait_recv()
    for i in range(8):
        ho[i * 64 : (i + 1) * 64, 2 * HEAD :] = b2[i].astype(F32).reshape(64, 2 * HEAD).astype(BF16)
    locals_[4].wait()
    both(s0, s1, 6)
    proj(xs, 0, 0)
    o1.second(0)
    o1.second(1)
    o0.second(0)
    proj(xs, 0, 1)
    proj(xs, 0, 2)
    o1.second(2)
    o0.second(1)
    proj(xs, 0, 3)
    qs[...] = acc[...].astype(BF16)
    o1.second(3)
    spatial(0, 0)
    o1.second(4)
    o0.second(2)
    spatial(0, 1)
    o1.second(5)
    spatial(1, 0)
    o0.second(3)
    spatial(1, 1)
    o1.second(6)

    order = (0, -1, 1, -2, 2, -3, 3, 4)
    xp, xm, x2 = (x + 1) % NX, (x + 3) % NX, (x + 2) % NX
    top, low = pl.ds(0, 32), pl.ds(32, 32)

    def ring(ref_from, ref_to, j, i, dev):
        return ref_from, ref_to, vs.at[j, i], vr.at[j, i], dev

    def project(j):
        n = (z + order[j]) % NZ
        o = nt_dot(ho[...], wo[n].reshape(SLAB, 4 * HEAD))
        p[j] = o.astype(BF16).reshape(NX, 2, 64, SLAB)
        send(*ring(p.at[j, :, 1 - core], c.at[j], j, 0, sibling))

    def pair(j):
        remote(*ring(c.at[j], c.at[j], j, 0, sibling)).wait_recv()
        d[j] = (p[j, :, core].astype(F32) + c[j].astype(F32)).astype(BF16)
        send(*ring(d.at[j, x2, top], e.at[j, 0], j, 1, dev_x(1)))
        send(*ring(d.at[j, x2, low], e.at[j, 1], j, 2, dev_x(-1)))

    def relay(j):
        remote(*ring(e.at[j, 0], e.at[j, 0], j, 1, dev_x(-1))).wait_recv()
        d[j, xp, 0:32] = (d[j, xp, 0:32].astype(F32) + e[j, 0].astype(F32)).astype(BF16)
        send(*ring(d.at[j, xp], f.at[j, 0], j, 3, dev_x(1)))
        remote(*ring(e.at[j, 1], e.at[j, 1], j, 2, dev_x(1))).wait_recv()
        d[j, xm, 32:64] = (d[j, xm, 32:64].astype(F32) + e[j, 1].astype(F32)).astype(BF16)
        send(*ring(d.at[j, xm], f.at[j, 1], j, 4, dev_x(-1)))

    def finish(j):
        remote(*ring(f.at[j, 0], f.at[j, 0], j, 3, dev_x(-1))).wait_recv()
        remote(*ring(f.at[j, 1], f.at[j, 1], j, 4, dev_x(1))).wait_recv()
        total = d[j, x].astype(F32) + f[j, 0].astype(F32) + f[j, 1].astype(F32)
        n = (z + order[j]) % NZ
        out_ref[:, pl.ds(pl.multiple_of(n * SLAB, SLAB), SLAB)] = total.astype(BF16)

    for j in range(11):
        if j == 3:
            o0.second(4)
        if j == 5:
            o0.second(5)
        if j == 7:
            o0.second(6)
        if j < 8:
            project(j)
        if 1 <= j <= 8:
            pair(j - 1)
        if 2 <= j <= 9:
            relay(j - 2)
        if 3 <= j:
            finish(j - 3)
    for copy in sent:
        copy.wait_send()
    lax.fori_loop(1, 64, end_tile, 0)


def shards(normed, qkv_weight, out_weight, segment_ids):
    rows = normed.reshape(PATCHES, WIDTH)
    tiles = normed.reshape(NZ, NY, 8, WIDTH)
    kinds = jnp.transpose(qkv_weight.reshape(PIECE, 2, 2 * QKV), (1, 0, 2))
    dma = pltpu.SemaphoreType.DMA
    out = pl.pallas_call(
        kernel,
        out_shape=jax.ShapeDtypeStruct((64, WIDTH), BF16),
        in_specs=[pl.BlockSpec(memory_space=pltpu.SMEM)] + [pl.BlockSpec(memory_space=pl.ANY)] * 4,
        out_specs=pl.BlockSpec(memory_space=pltpu.VMEM),
        scratch_shapes=[
            pltpu.VMEM((PATCHES, WIDTH), BF16),
            pltpu.VMEM((PATCHES, WIDTH), BF16),
            pltpu.VMEM((2, NZ, NY, PIECE, 2 * QKV), BF16),
            pltpu.VMEM((NZ, NY, PIECE, 4 * HEAD), BF16),
            pltpu.VMEM((NZ, NY, 8, SLAB), BF16),
            pltpu.VMEM((8, NZ, NY, 8, SLAB), BF16),
            pltpu.VMEM((PATCHES, 2 * QKV), F32),
            pltpu.VMEM((PATCHES, 2 * QKV), BF16),
            pltpu.VMEM((PATCHES, 2 * QKV), BF16),
            pltpu.VMEM((NZ, NY, 8, 2 * HEAD), BF16),
            pltpu.VMEM((NZ, NY, 8, 2 * HEAD), BF16),
            pltpu.VMEM((NZ, NY, 8, 2 * HEAD), BF16),
            pltpu.VMEM((PATCHES, 4 * HEAD), BF16),
            pltpu.VMEM((8, NX, 2, 64, SLAB), BF16),
            pltpu.VMEM((8, NX, 64, SLAB), BF16),
            pltpu.VMEM((8, NX, 64, SLAB), BF16),
            pltpu.VMEM((8, 2, 32, SLAB), BF16),
            pltpu.VMEM((8, 2, 64, SLAB), BF16),
            pltpu.VMEM((PATCHES, HEAD), jnp.int32),
            pltpu.VMEM((8, PATCHES), jnp.int32),
            dma((6, 21)), dma((6, 21)),
            dma((63,)), dma((63,)),
            dma((8,)), dma((8,)),
            dma((14,)), dma((14,)),
            dma((8, 5)), dma((8, 5)),
            dma((8,)),
        ],
        compiler_params=pltpu.CompilerParams(
            collective_id=0, has_side_effects=True, vmem_limit_bytes=60 * 2**20
        ),
        name="whole",
    )(segment_ids, rows, tiles, kinds, out_weight)
    return out.reshape(1, 64, WIDTH)


def solution(mesh):
    return jax.shard_map(
        shards,
        mesh=mesh,
        in_specs=(P("fsdp", None, None), P("fsdp", "st", None), P("fsdp", "st"), P()),
        out_specs=P("fsdp", "st", None),
        check_vma=False,
    )
```

```python
import functools
import math

import jax
import jax.numpy as jnp
from jax import lax
from jax.experimental import pallas as pl
from jax.experimental.pallas import tpu as pltpu
from jax.sharding import PartitionSpec as P

HEAD = 128
MESH = pl.DeviceIdType.MESH
NZ = NY = 8
NX = 4
PIECE = 48
QKV = 3 * HEAD
SLAB = 384
PATCHES = 512
WIDTH = 3072
UP = ((-1, 0), (-1, 1), (-2, 0), (-2, 1), (-3, 0), (-3, 1), (-4, 0))
DOWN = ((1, 1), (1, 0), (2, 1), (2, 0), (3, 1), (3, 0), (4, 1))
F32 = jnp.float32
BF16 = jnp.bfloat16


def nt_dot(a, b):
    return lax.dot_general(a, b, (((1,), (1,)), ((), ())), preferred_element_type=F32)


def nn_dot(a, b):
    return lax.dot_general(a, b, (((1,), (0,)), ((), ())), preferred_element_type=F32)


def softmax_rows(scores):
    top = jnp.max(scores, axis=-1, keepdims=True)
    expo = jnp.exp(scores - top)
    return expo * (1.0 / jnp.sum(expo, axis=-1, keepdims=True))


def kernel(
    seg_ref, x_ref, x4_ref, wq_ref, wo_ref, out_ref,
    xs, xt, w, wo, stage, a, acc, qt, qs, ot, b1, b2, ho, p, c, d, e, f, idc, idr,
    gs, gr, ns, nr, xsem, xrec, ts, tr, vs, vr, loc,
):
    st, fs = lax.axis_index("st"), lax.axis_index("fsdp")
    x, core = st // 2, st % 2
    z, y = fs // NY, fs % NY
    scale = 1.0 / math.sqrt(HEAD)
    sent = []

    def dev_y(k):
        return (st, z * NY + (y + k) % NY)

    def dev_z(k):
        return (st, ((z + k) % NZ) * NY + y)

    def dev_x(k):
        return (((x + k) % NX) * 2 + core, fs)

    sibling = (x * 2 + 1 - core, fs)

    def remote(src, dst, ssem, rsem, dev):
        return pltpu.make_async_remote_copy(
            src_ref=src, dst_ref=dst, send_sem=ssem, recv_sem=rsem, device_id=dev, device_id_type=MESH
        )

    def send(*args):
        copy = remote(*args)
        copy.start()
        sent.append(copy)

    barrier = pltpu.get_barrier_semaphore()

    def greet(k, _):
        pl.semaphore_signal(barrier, inc=1, device_id=(st, (fs + k) % 64), device_id_type=MESH)
        return 0

    lax.fori_loop(1, 64, greet, 0)
    for dev in (dev_x(1), dev_x(-1), sibling):
        pl.semaphore_signal(barrier, inc=1, device_id=dev, device_id_type=MESH)

    cols = pl.ds(pl.multiple_of(st * SLAB, SLAB), SLAB)
    locals_ = [
        pltpu.make_async_copy(x4_ref.at[:, :, :, cols], stage, loc.at[0]),
        pltpu.make_async_copy(wo_ref, wo.at[z, y], loc.at[1]),
        pltpu.make_async_copy(wq_ref.at[0], w.at[0, z, y], loc.at[2]),
        pltpu.make_async_copy(wq_ref.at[1], w.at[1, z, y], loc.at[3]),
        pltpu.make_async_copy(x_ref, xs, loc.at[4]),
    ]
    for cp in locals_:
        cp.start()

    sub8 = lax.broadcasted_iota(jnp.int32, (8, HEAD), 0)
    lane = lax.broadcasted_iota(jnp.int32, (8, PATCHES), 1)
    row = jnp.zeros((8, PATCHES), jnp.int32)
    for t in range(64):
        sid = seg_ref[t]
        idc[t * 8 : (t + 1) * 8, :] = sub8 + sid * 8
        row = jnp.where(lane // 8 == t, sid * 8, row)
    idr[...] = row + lane % 8

    for cp in locals_[:4]:
        cp.wait()
    own_tile = pltpu.make_async_copy(stage.at[z, y], a.at[st, z, y], loc.at[5])
    own_tile.start()
    own_tile.wait()
    pl.semaphore_wait(barrier, 66)

    class Stream:
        def __init__(self, number, y_first, flip, view):
            self.n, self.y_first, self.flip, self.view = number, y_first, flip, view
            self.ac, self.bc = (y, z) if y_first else (z, y)
            self.da, self.db = (dev_y, dev_z) if y_first else (dev_z, dev_y)

        def piece(self, at):
            return self.view(self.bc, at) if self.y_first else self.view(at, self.bc)

        def slab(self, bt, sub):
            four = pl.ds(4 * sub, 4)
            return self.view(bt, four) if self.y_first else self.view(four, bt)

        def sems(self, i):
            return gs.at[self.n, i], gr.at[self.n, i]

        def first_own(self):
            right = 1 if not self.flip else -1
            own = self.piece(self.ac)
            send(own, own, *self.sems(0), self.da(right))
            send(own, own, *self.sems(4), self.da(-right))

        def first(self, k):
            right = 1 if not self.flip else -1
            for way, base, last in ((right, 0, 4), (-right, 4, 3)):
                if k <= last:
                    got = self.piece((self.ac - way * k) % 8)
                    remote(got, got, *self.sems(base + k - 1), self.da(-way)).wait_recv()
                    if k < last:
                        send(got, got, *self.sems(base + k), self.da(way))

        def second_own(self):
            for sub in (0, 1):
                for way, base, chain in ((1, 7, UP), (-1, 14, DOWN)):
                    blk = self.slab(self.bc, chain[sub][1])
                    send(blk, blk, *self.sems(base + sub), self.db(way))

        def second(self, i):
            for way, base, chain in ((1, 7, UP), (-1, 14, DOWN)):
                off, sub = chain[i]
                got = self.slab((self.bc + off) % 8, sub)
                remote(got, got, *self.sems(base + i), self.db(-way)).wait_recv()
                if i <= 4:
                    send(got, got, *self.sems(base + i + 2), self.db(way))

    def head_stream(number, kind, h, y_first, flip):
        return Stream(number, y_first, flip, lambda zi, yi: w.at[kind, zi, yi, ..., pl.ds(h * QKV, QKV)])

    t0 = head_stream(0, 1, 0, True, False)
    t1 = head_stream(1, 1, 1, False, True)
    s0 = head_stream(2, 0, 0, True, True)
    s1 = head_stream(3, 0, 1, False, False)
    o0 = Stream(4, True, False, lambda zi, yi: wo.at[zi, yi, ..., pl.ds(0, 32), :])
    o1 = Stream(5, False, True, lambda zi, yi: wo.at[zi, yi, ..., pl.ds(32, 16), :])

    def both(one, two, i):
        one.second(i)
        two.second(i)

    t0.first_own()
    t1.first_own()

    def tile_out(k):
        to = (fs + k) % 64
        return remote(stage.at[to // NY, to % NY], a.at[st, z, y], ns.at[k - 1], nr.at[k - 1], (st, to))

    def tile_in(k):
        to = (fs + 64 - k) % 64
        got = a.at[st, to // NY, to % NY]
        return remote(got, got, ns.at[k - 1], nr.at[k - 1], (st, to))

    def start_tile(k, _):
        tile_out(k).start()
        return 0

    def await_tile(k, _):
        tile_in(k).wait_recv()
        return 0

    def end_tile(k, _):
        tile_out(k).wait_send()
        return 0

    others = (s0, s1, o1, o0)
    for s in others:
        s.first_own()
    for k in range(1, 5):
        lax.fori_loop(16 * k - 15, min(16 * k + 1, 64), start_tile, 0)
        for s in (t0, t1, *others):
            s.first(k)
    t0.second_own()
    t1.second_own()

    def assemble(sl):
        def body(i, _):
            v = a[sl, i].astype(F32).reshape(64, SLAB).astype(BF16)
            rows = pl.ds(pl.multiple_of(i * 64, 64), 64)
            xt[rows, pl.ds(pl.multiple_of(sl * SLAB, SLAB), SLAB)] = v
            return 0

        lax.fori_loop(0, 8, body, 0)

    sl_m, sl_p, sl_2 = (((x + k) % NX) * 2 + core for k in (3, 1, 2))
    lo, hi = pl.ds(0, 4), pl.ds(4, 4)

    def xmove(ref, i, dev):
        return ref, ref, xsem.at[i], xrec.at[i], dev

    def from_sibling(i, sl):
        other = sl + 1 - 2 * core
        remote(*xmove(a.at[other], 4 + i, sibling)).wait_recv()
        assemble(other)

    lax.fori_loop(1, 64, await_tile, 0)
    send(*xmove(a.at[st], 0, dev_x(1)))
    send(*xmove(a.at[st], 1, dev_x(-1)))
    send(*xmove(a.at[st], 4, sibling))
    both(t0, t1, 0)
    assemble(st)
    both(t0, t1, 1)
    from_sibling(0, st)
    both(t0, t1, 2)
    remote(*xmove(a.at[sl_m], 0, dev_x(-1))).wait_recv()
    send(*xmove(a.at[sl_m, lo], 2, dev_x(1)))
    send(*xmove(a.at[sl_m], 5, sibling))
    remote(*xmove(a.at[sl_p], 1, dev_x(1))).wait_recv()
    send(*xmove(a.at[sl_p, hi], 3, dev_x(-1)))
    send(*xmove(a.at[sl_p], 6, sibling))
    assemble(sl_m)
    both(t0, t1, 3)
    assemble(sl_p)
    both(t0, t1, 4)
    s0.second_own()
    s1.second_own()
    remote(*xmove(a.at[sl_2, lo], 2, dev_x(-1))).wait_recv()
    remote(*xmove(a.at[sl_2, hi], 3, dev_x(1))).wait_recv()
    send(*xmove(a.at[sl_2], 7, sibling))
    assemble(sl_2)
    from_sibling(1, sl_m)
    both(t0, t1, 5)
    from_sibling(2, sl_p)
    from_sibling(3, sl_2)
    both(t0, t1, 6)

    def proj(rows, kind, i):
        part = nn_dot(rows[:, i * 2 * SLAB : (i + 1) * 2 * SLAB], w[kind, 2 * i : 2 * i + 2].reshape(2 * SLAB, 2 * QKV))
        acc[...] = part if i == 0 else acc[...] + part

    def proj_slab(off, first=False):
        n = (z + off) % NZ
        part = nn_dot(
            xs[:, pl.ds(pl.multiple_of(n * SLAB, SLAB), SLAB)], w[0, n, :, :, 0:QKV].reshape(SLAB, QKV)
        )
        acc[:, 0:QKV] = part if first else acc[:, 0:QKV] + part

    def proj_second(i):
        part = nn_dot(
            xs[:, i * 2 * SLAB : (i + 1) * 2 * SLAB],
            w[0, 2 * i : 2 * i + 2, :, :, QKV:].reshape(2 * SLAB, QKV),
        )
        acc[:, QKV:] = part if i == 0 else acc[:, QKV:] + part

    def temporal(h):
        base = h * QKV
        for b, start in enumerate((0, 64, 192, 256)):
            rows, keys = pl.ds(b * 128, 128), pl.ds(start, 256)
            s = nt_dot(qt[rows, base : base + HEAD], qt[keys, base + HEAD : base + 2 * HEAD]) * scale
            same = idc[rows, 0:1] == idr[0:1, keys]
            wt = softmax_rows(jnp.where(same, s, -1e30)).astype(BF16)
            o = nn_dot(wt, qt[keys, base + 2 * HEAD : base + QKV])
            ot[2 * b : 2 * b + 2, :, :, h * HEAD : (h + 1) * HEAD] = o.reshape(2, 8, 8, HEAD).astype(BF16)

    def spatial(h, half):
        base = h * QKV
        rows = pl.ds(half * 256, 256)
        s = nt_dot(qs[rows, base : base + HEAD], qs[:, base + HEAD : base + 2 * HEAD]) * scale
        o = nn_dot(softmax_rows(s).astype(BF16), qs[:, base + 2 * HEAD : base + QKV])
        ho[rows, h * HEAD : (h + 1) * HEAD] = o.astype(BF16)

    proj(xt, 1, 0)
    proj(xt, 1, 1)
    both(s0, s1, 0)
    proj(xt, 1, 2)
    proj(xt, 1, 3)
    qt[...] = acc[...].astype(BF16)
    both(s0, s1, 1)
    temporal(0)
    both(s0, s1, 2)
    temporal(1)
    for k in range(1, 8):
        send(ot.at[(z + k) % NZ], b1.at[z], ts.at[k - 1], tr.at[k - 1], dev_z(k))
    back = pltpu.make_async_copy(ot.at[z], b1.at[z], loc.at[6])
    back.start()
    locals_[4].wait()
    both(s0, s1, 3)
    proj_slab(0, True)
    back.wait()
    for k in range(1, 8):
        got = b1.at[(z - k) % NZ]
        remote(got, got, ts.at[k - 1], tr.at[k - 1], dev_z(-k)).wait_recv()
    for k in range(1, 8):
        send(b1.at[:, (y + k) % NY], b2.at[:, y], ts.at[6 + k], tr.at[6 + k], dev_y(k))
    back2 = pltpu.make_async_copy(b1.at[:, y], b2.at[:, y], loc.at[7])
    back2.start()
    both(s0, s1, 4)
    o1.second_own()
    o0.second_own()
    proj_slab(-1)
    proj_slab(1)
    both(s0, s1, 5)
    proj_slab(-2)
    proj_slab(2)
    o1.second(0)
    both(s0, s1, 6)
    o1.second(1)
    o0.second(0)
    proj_slab(-3)
    proj_slab(3)
    o1.second(2)
    proj_slab(4)
    o1.second(3)
    o0.second(1)
    proj_second(0)
    proj_second(1)
    o1.second(4)
    proj_second(2)
    proj_second(3)
    qs[...] = acc[...].astype(BF16)
    o1.second(5)
    o0.second(2)
    spatial(0, 0)
    spatial(0, 1)
    o1.second(6)
    back2.wait()
    for k in range(1, 8):
        got = b2.at[:, (y - k) % NY]
        remote(got, got, ts.at[6 + k], tr.at[6 + k], dev_y(-k)).wait_recv()
    for i in range(8):
        ho[i * 64 : (i + 1) * 64, 2 * HEAD :] = b2[i].astype(F32).reshape(64, 2 * HEAD).astype(BF16)
    o0.second(3)
    spatial(1, 0)
    spatial(1, 1)

    order = (0, -1, 1, -2, 2, -3, 3, 4)
    xp, xm, x2 = (x + 1) % NX, (x + 3) % NX, (x + 2) % NX
    top, low = pl.ds(0, 32), pl.ds(32, 32)

    def ring(ref_from, ref_to, j, i, dev):
        return ref_from, ref_to, vs.at[j, i], vr.at[j, i], dev

    def project(j):
        n = (z + order[j]) % NZ
        o = nt_dot(ho[...], wo[n].reshape(SLAB, 4 * HEAD))
        p[j] = o.astype(BF16).reshape(NX, 2, 64, SLAB)
        send(*ring(p.at[j, :, 1 - core], c.at[j], j, 0, sibling))

    def pair(j):
        remote(*ring(c.at[j], c.at[j], j, 0, sibling)).wait_recv()
        d[j] = (p[j, :, core].astype(F32) + c[j].astype(F32)).astype(BF16)
        send(*ring(d.at[j, x2, top], e.at[j, 0], j, 1, dev_x(1)))
        send(*ring(d.at[j, x2, low], e.at[j, 1], j, 2, dev_x(-1)))

    def relay(j):
        remote(*ring(e.at[j, 0], e.at[j, 0], j, 1, dev_x(-1))).wait_recv()
        d[j, xp, 0:32] = (d[j, xp, 0:32].astype(F32) + e[j, 0].astype(F32)).astype(BF16)
        send(*ring(d.at[j, xp], f.at[j, 0], j, 3, dev_x(1)))
        remote(*ring(e.at[j, 1], e.at[j, 1], j, 2, dev_x(1))).wait_recv()
        d[j, xm, 32:64] = (d[j, xm, 32:64].astype(F32) + e[j, 1].astype(F32)).astype(BF16)
        send(*ring(d.at[j, xm], f.at[j, 1], j, 4, dev_x(-1)))

    def finish(j):
        remote(*ring(f.at[j, 0], f.at[j, 0], j, 3, dev_x(-1))).wait_recv()
        remote(*ring(f.at[j, 1], f.at[j, 1], j, 4, dev_x(1))).wait_recv()
        total = d[j, x].astype(F32) + f[j, 0].astype(F32) + f[j, 1].astype(F32)
        n = (z + order[j]) % NZ
        out_ref[:, pl.ds(pl.multiple_of(n * SLAB, SLAB), SLAB)] = total.astype(BF16)

    for j in range(14):
        if j in (1, 4, 6):
            o0.second({1: 4, 4: 5, 6: 6}[j])
        if j < 8:
            project(j)
        if 2 <= j <= 9:
            pair(j - 2)
        if 4 <= j <= 11:
            relay(j - 4)
        if 6 <= j:
            finish(j - 6)
    for copy in sent:
        copy.wait_send()
    lax.fori_loop(1, 64, end_tile, 0)


def shards(normed, qkv_weight, out_weight, segment_ids):
    rows = normed.reshape(PATCHES, WIDTH)
    tiles = normed.reshape(NZ, NY, 8, WIDTH)
    kinds = jnp.transpose(qkv_weight.reshape(PIECE, 2, 2 * QKV), (1, 0, 2))
    dma = pltpu.SemaphoreType.DMA
    out = pl.pallas_call(
        kernel,
        out_shape=jax.ShapeDtypeStruct((64, WIDTH), BF16),
        in_specs=[pl.BlockSpec(memory_space=pltpu.SMEM)] + [pl.BlockSpec(memory_space=pl.ANY)] * 4,
        out_specs=pl.BlockSpec(memory_space=pltpu.VMEM),
        scratch_shapes=[
            pltpu.VMEM((PATCHES, WIDTH), BF16),
            pltpu.VMEM((PATCHES, WIDTH), BF16),
            pltpu.VMEM((2, NZ, NY, PIECE, 2 * QKV), BF16),
            pltpu.VMEM((NZ, NY, PIECE, 4 * HEAD), BF16),
            pltpu.VMEM((NZ, NY, 8, SLAB), BF16),
            pltpu.VMEM((8, NZ, NY, 8, SLAB), BF16),
            pltpu.VMEM((PATCHES, 2 * QKV), F32),
            pltpu.VMEM((PATCHES, 2 * QKV), BF16),
            pltpu.VMEM((PATCHES, 2 * QKV), BF16),
            pltpu.VMEM((NZ, NY, 8, 2 * HEAD), BF16),
            pltpu.VMEM((NZ, NY, 8, 2 * HEAD), BF16),
            pltpu.VMEM((NZ, NY, 8, 2 * HEAD), BF16),
            pltpu.VMEM((PATCHES, 4 * HEAD), BF16),
            pltpu.VMEM((8, NX, 2, 64, SLAB), BF16),
            pltpu.VMEM((8, NX, 64, SLAB), BF16),
            pltpu.VMEM((8, NX, 64, SLAB), BF16),
            pltpu.VMEM((8, 2, 32, SLAB), BF16),
            pltpu.VMEM((8, 2, 64, SLAB), BF16),
            pltpu.VMEM((PATCHES, HEAD), jnp.int32),
            pltpu.VMEM((8, PATCHES), jnp.int32),
            dma((6, 21)), dma((6, 21)),
            dma((63,)), dma((63,)),
            dma((8,)), dma((8,)),
            dma((14,)), dma((14,)),
            dma((8, 5)), dma((8, 5)),
            dma((8,)),
        ],
        compiler_params=pltpu.CompilerParams(
            collective_id=0, has_side_effects=True, vmem_limit_bytes=60 * 2**20
        ),
        name="whole",
    )(segment_ids, rows, tiles, kinds, out_weight)
    return out.reshape(1, 64, WIDTH)


def solution(mesh):
    return jax.shard_map(
        shards,
        mesh=mesh,
        in_specs=(P("fsdp", None, None), P("fsdp", "st", None), P("fsdp", "st"), P()),
        out_specs=P("fsdp", "st", None),
        check_vma=False,
    )
```

```python
import functools
import math

import jax
import jax.numpy as jnp
from jax import lax
from jax.experimental import pallas as pl
from jax.experimental.pallas import tpu as pltpu
from jax.sharding import PartitionSpec as P

HEAD = 128
MESH = pl.DeviceIdType.MESH
NZ = NY = 8
NX = 4
PIECE = 48
QKV = 3 * HEAD
SLAB = 384
PATCHES = 512
WIDTH = 3072
UP = ((-1, 0), (-1, 1), (-2, 0), (-2, 1), (-3, 0), (-3, 1), (-4, 0))
DOWN = ((1, 1), (1, 0), (2, 1), (2, 0), (3, 1), (3, 0), (4, 1))
SPREAD = (1, 7, 2, 6, 3, 5, 4)
F32 = jnp.float32
BF16 = jnp.bfloat16


def nt_dot(a, b):
    return lax.dot_general(a, b, (((1,), (1,)), ((), ())), preferred_element_type=F32)


def nn_dot(a, b):
    return lax.dot_general(a, b, (((1,), (0,)), ((), ())), preferred_element_type=F32)


def softmax_rows(scores):
    top = jnp.max(scores, axis=-1, keepdims=True)
    expo = jnp.exp(scores - top)
    return expo * (1.0 / jnp.sum(expo, axis=-1, keepdims=True))


def kernel(
    seg_ref, x_ref, x4_ref, wq_ref, wo_ref, out_ref,
    xs, xt, w, wo, stage, a, acc, qt, qs, ot, b1, b2, ho, p, c, d, e, f, idc, idr, raw,
    gs, gr, ns, nr, xsem, xrec, ts, tr, vs, vr, loc,
):
    st, fs = lax.axis_index("st"), lax.axis_index("fsdp")
    x, core = st // 2, st % 2
    z, y = fs // NY, fs % NY
    scale = 1.0 / math.sqrt(HEAD)
    sent = []

    def dev_y(k):
        return (st, z * NY + (y + k) % NY)

    def dev_z(k):
        return (st, ((z + k) % NZ) * NY + y)

    def dev_x(k):
        return (((x + k) % NX) * 2 + core, fs)

    sibling = (x * 2 + 1 - core, fs)

    def remote(src, dst, ssem, rsem, dev):
        return pltpu.make_async_remote_copy(
            src_ref=src, dst_ref=dst, send_sem=ssem, recv_sem=rsem, device_id=dev, device_id_type=MESH
        )

    def send(*args):
        copy = remote(*args)
        copy.start()
        sent.append(copy)

    barrier = pltpu.get_barrier_semaphore()

    def greet(k, _):
        pl.semaphore_signal(barrier, inc=1, device_id=(st, (fs + k) % 64), device_id_type=MESH)
        return 0

    lax.fori_loop(1, 64, greet, 0)
    for dev in (dev_x(1), dev_x(-1), sibling):
        pl.semaphore_signal(barrier, inc=1, device_id=dev, device_id_type=MESH)

    cols = pl.ds(pl.multiple_of(st * SLAB, SLAB), SLAB)
    locals_ = [
        pltpu.make_async_copy(x4_ref.at[:, :, :, cols], stage, loc.at[0]),
        pltpu.make_async_copy(wo_ref, wo.at[z, y], loc.at[1]),
        pltpu.make_async_copy(wq_ref, raw, loc.at[2]),
        pltpu.make_async_copy(x_ref, xs, loc.at[4]),
    ]
    for cp in locals_:
        cp.start()

    sub8 = lax.broadcasted_iota(jnp.int32, (8, HEAD), 0)
    lane = lax.broadcasted_iota(jnp.int32, (8, PATCHES), 1)
    row = jnp.zeros((8, PATCHES), jnp.int32)
    for t in range(64):
        sid = seg_ref[t]
        idc[t * 8 : (t + 1) * 8, :] = sub8 + sid * 8
        row = jnp.where(lane // 8 == t, sid * 8, row)
    idr[...] = row + lane % 8

    for cp in locals_[:3]:
        cp.wait()
    for h in range(4):
        w[h // 2, z, y, :, h % 2 * QKV : (h % 2 + 1) * QKV] = raw[:, h, :]
    own_tile = pltpu.make_async_copy(stage.at[z, y], a.at[st, z, y], loc.at[5])
    own_tile.start()
    own_tile.wait()
    pl.semaphore_wait(barrier, 66)

    class Stream:
        def __init__(self, number, y_first, flip, view):
            self.n, self.y_first, self.flip, self.view = number, y_first, flip, view
            self.ac, self.bc = (y, z) if y_first else (z, y)
            self.da, self.db = (dev_y, dev_z) if y_first else (dev_z, dev_y)

        def piece(self, at):
            return self.view(self.bc, at) if self.y_first else self.view(at, self.bc)

        def slab(self, bt, sub):
            four = pl.ds(4 * sub, 4)
            return self.view(bt, four) if self.y_first else self.view(four, bt)

        def sems(self, i):
            return gs.at[self.n, i], gr.at[self.n, i]

        def first_own(self):
            right = 1 if not self.flip else -1
            own = self.piece(self.ac)
            send(own, own, *self.sems(0), self.da(right))
            send(own, own, *self.sems(4), self.da(-right))

        def first(self, k):
            right = 1 if not self.flip else -1
            for way, base, last in ((right, 0, 4), (-right, 4, 3)):
                if k <= last:
                    got = self.piece((self.ac - way * k) % 8)
                    remote(got, got, *self.sems(base + k - 1), self.da(-way)).wait_recv()
                    if k < last:
                        send(got, got, *self.sems(base + k), self.da(way))

        def second_own(self):
            for sub in (0, 1):
                for way, base, chain in ((1, 7, UP), (-1, 14, DOWN)):
                    blk = self.slab(self.bc, chain[sub][1])
                    send(blk, blk, *self.sems(base + sub), self.db(way))

        def second(self, i):
            for way, base, chain in ((1, 7, UP), (-1, 14, DOWN)):
                off, sub = chain[i]
                got = self.slab((self.bc + off) % 8, sub)
                remote(got, got, *self.sems(base + i), self.db(-way)).wait_recv()
                if i <= 4:
                    send(got, got, *self.sems(base + i + 2), self.db(way))

    def head_stream(number, kind, h, y_first, flip):
        return Stream(number, y_first, flip, lambda zi, yi: w.at[kind, zi, yi, ..., pl.ds(h * QKV, QKV)])

    t0 = head_stream(0, 1, 0, True, False)
    t1 = head_stream(1, 1, 1, False, True)
    s0 = head_stream(2, 0, 0, True, True)
    s1 = head_stream(3, 0, 1, False, False)
    o0 = Stream(4, True, False, lambda zi, yi: wo.at[zi, yi, ..., pl.ds(0, 32), :])
    o1 = Stream(5, False, True, lambda zi, yi: wo.at[zi, yi, ..., pl.ds(32, 16), :])

    def both(one, two, i):
        one.second(i)
        two.second(i)

    t0.first_own()
    t1.first_own()

    def tile_out(k):
        to = (fs + 27 * k) % 64
        return remote(stage.at[to // NY, to % NY], a.at[st, z, y], ns.at[k - 1], nr.at[k - 1], (st, to))

    def tile_in(k):
        to = (fs + 37 * k) % 64
        got = a.at[st, to // NY, to % NY]
        return remote(got, got, ns.at[k - 1], nr.at[k - 1], (st, to))

    def start_tile(k, _):
        tile_out(k).start()
        return 0

    def await_tile(k, _):
        tile_in(k).wait_recv()
        return 0

    def end_tile(k, _):
        tile_out(k).wait_send()
        return 0

    others = (s0, s1, o1, o0)
    for s in others:
        s.first_own()
    for k in range(1, 5):
        lax.fori_loop(16 * k - 15, min(16 * k + 1, 64), start_tile, 0)
        t0.first(k)
        t1.first(k)
    t0.second_own()
    t1.second_own()

    def first_others(k):
        for s in others:
            s.first(k)

    first_others(1)
    first_others(2)

    def assemble(sl):
        def body(i, _):
            v = a[sl, i].astype(F32).reshape(64, SLAB).astype(BF16)
            rows = pl.ds(pl.multiple_of(i * 64, 64), 64)
            xt[rows, pl.ds(pl.multiple_of(sl * SLAB, SLAB), SLAB)] = v
            return 0

        lax.fori_loop(0, 8, body, 0)

    sl_m, sl_p, sl_2 = (((x + k) % NX) * 2 + core for k in (3, 1, 2))
    lo, hi = pl.ds(0, 4), pl.ds(4, 4)

    def xmove(ref, i, dev):
        return ref, ref, xsem.at[i], xrec.at[i], dev

    def from_sibling(i, sl):
        other = sl + 1 - 2 * core
        remote(*xmove(a.at[other], 4 + i, sibling)).wait_recv()
        assemble(other)

    lax.fori_loop(1, 64, await_tile, 0)
    send(*xmove(a.at[st], 0, dev_x(1)))
    send(*xmove(a.at[st], 1, dev_x(-1)))
    send(*xmove(a.at[st], 4, sibling))
    both(t0, t1, 0)
    first_others(3)
    assemble(st)
    both(t0, t1, 1)
    first_others(4)
    from_sibling(0, st)
    both(t0, t1, 2)
    remote(*xmove(a.at[sl_m], 0, dev_x(-1))).wait_recv()
    send(*xmove(a.at[sl_m, lo], 2, dev_x(1)))
    send(*xmove(a.at[sl_m], 5, sibling))
    remote(*xmove(a.at[sl_p], 1, dev_x(1))).wait_recv()
    send(*xmove(a.at[sl_p, hi], 3, dev_x(-1)))
    send(*xmove(a.at[sl_p], 6, sibling))
    assemble(sl_m)
    both(t0, t1, 3)
    assemble(sl_p)
    both(t0, t1, 4)
    s0.second_own()
    s1.second_own()
    remote(*xmove(a.at[sl_2, lo], 2, dev_x(-1))).wait_recv()
    remote(*xmove(a.at[sl_2, hi], 3, dev_x(1))).wait_recv()
    send(*xmove(a.at[sl_2], 7, sibling))
    assemble(sl_2)
    from_sibling(1, sl_m)
    both(t0, t1, 5)
    from_sibling(2, sl_p)
    from_sibling(3, sl_2)
    both(t0, t1, 6)

    def proj(rows, kind, i):
        part = nn_dot(rows[:, i * 2 * SLAB : (i + 1) * 2 * SLAB], w[kind, 2 * i : 2 * i + 2].reshape(2 * SLAB, 2 * QKV))
        acc[...] = part if i == 0 else acc[...] + part

    def proj_slab(off, first=False):
        n = (z + off) % NZ
        part = nn_dot(
            xs[:, pl.ds(pl.multiple_of(n * SLAB, SLAB), SLAB)], w[0, n, :, :, 0:QKV].reshape(SLAB, QKV)
        )
        acc[:, 0:QKV] = part if first else acc[:, 0:QKV] + part

    def proj_second(i):
        part = nn_dot(
            xs[:, i * 2 * SLAB : (i + 1) * 2 * SLAB],
            w[0, 2 * i : 2 * i + 2, :, :, QKV:].reshape(2 * SLAB, QKV),
        )
        acc[:, QKV:] = part if i == 0 else acc[:, QKV:] + part

    def temporal(h):
        base = h * QKV
        for b, start in enumerate((0, 64, 192, 256)):
            rows, keys = pl.ds(b * 128, 128), pl.ds(start, 256)
            s = nt_dot(qt[rows, base : base + HEAD], qt[keys, base + HEAD : base + 2 * HEAD]) * scale
            same = idc[rows, 0:1] == idr[0:1, keys]
            wt = softmax_rows(jnp.where(same, s, -1e30)).astype(BF16)
            o = nn_dot(wt, qt[keys, base + 2 * HEAD : base + QKV])
            ot[2 * b : 2 * b + 2, :, :, h * HEAD : (h + 1) * HEAD] = o.reshape(2, 8, 8, HEAD).astype(BF16)

    def spatial(h, half):
        base = h * QKV
        rows = pl.ds(half * 256, 256)
        s = nt_dot(qs[rows, base : base + HEAD], qs[:, base + HEAD : base + 2 * HEAD]) * scale
        o = nn_dot(softmax_rows(s).astype(BF16), qs[:, base + 2 * HEAD : base + QKV])
        ho[rows, h * HEAD : (h + 1) * HEAD] = o.astype(BF16)

    proj(xt, 1, 0)
    both(s0, s1, 0)
    proj(xt, 1, 1)
    proj(xt, 1, 2)
    proj(xt, 1, 3)
    qt[...] = acc[...].astype(BF16)
    both(s0, s1, 1)
    temporal(0)
    temporal(1)
    for k in SPREAD:
        send(ot.at[(z + k) % NZ], b1.at[z], ts.at[k - 1], tr.at[k - 1], dev_z(k))
    back = pltpu.make_async_copy(ot.at[z], b1.at[z], loc.at[6])
    back.start()
    locals_[3].wait()
    both(s0, s1, 2)
    proj_slab(0, True)
    back.wait()
    for k in range(1, 8):
        got = b1.at[(z - k) % NZ]
        remote(got, got, ts.at[k - 1], tr.at[k - 1], dev_z(-k)).wait_recv()
    for k in SPREAD:
        send(b1.at[:, (y + k) % NY], b2.at[:, y], ts.at[6 + k], tr.at[6 + k], dev_y(k))
    back2 = pltpu.make_async_copy(b1.at[:, y], b2.at[:, y], loc.at[7])
    back2.start()
    both(s0, s1, 3)
    both(s0, s1, 4)
    o1.second_own()
    o0.second_own()
    proj_slab(-1)
    proj_slab(1)
    both(s0, s1, 5)
    proj_slab(-2)
    proj_slab(2)
    o1.second(0)
    both(s0, s1, 6)
    o1.second(1)
    proj_slab(-3)
    proj_slab(3)
    proj_slab(4)
    o1.second(2)
    o0.second(0)
    proj_second(0)
    proj_second(1)
    o1.second(3)
    proj_second(2)
    proj_second(3)
    qs[...] = acc[...].astype(BF16)
    o1.second(4)
    o0.second(1)
    spatial(0, 0)
    spatial(0, 1)
    o1.second(5)
    spatial(1, 0)
    spatial(1, 1)
    back2.wait()
    for k in range(1, 8):
        got = b2.at[:, (y - k) % NY]
        remote(got, got, ts.at[6 + k], tr.at[6 + k], dev_y(-k)).wait_recv()
    for i in range(8):
        ho[i * 64 : (i + 1) * 64, 2 * HEAD :] = b2[i].astype(F32).reshape(64, 2 * HEAD).astype(BF16)
    o0.second(2)
    o1.second(6)

    order = (0, -1, 1, -2, 2, -3, 3, 4)
    xp, xm, x2 = (x + 1) % NX, (x + 3) % NX, (x + 2) % NX
    top, low = pl.ds(0, 32), pl.ds(32, 32)

    def ring(ref_from, ref_to, j, i, dev):
        return ref_from, ref_to, vs.at[j, i], vr.at[j, i], dev

    def project(j):
        n = (z + order[j]) % NZ
        o = nt_dot(ho[...], wo[n].reshape(SLAB, 4 * HEAD))
        p[j] = o.astype(BF16).reshape(NX, 2, 64, SLAB)
        send(*ring(p.at[j, :, 1 - core], c.at[j], j, 0, sibling))

    def pair(j):
        remote(*ring(c.at[j], c.at[j], j, 0, sibling)).wait_recv()
        d[j] = (p[j, :, core].astype(F32) + c[j].astype(F32)).astype(BF16)
        send(*ring(d.at[j, x2, top], e.at[j, 0], j, 1, dev_x(1)))
        send(*ring(d.at[j, x2, low], e.at[j, 1], j, 2, dev_x(-1)))

    def relay(j):
        remote(*ring(e.at[j, 0], e.at[j, 0], j, 1, dev_x(-1))).wait_recv()
        d[j, xp, 0:32] = (d[j, xp, 0:32].astype(F32) + e[j, 0].astype(F32)).astype(BF16)
        send(*ring(d.at[j, xp], f.at[j, 0], j, 3, dev_x(1)))
        remote(*ring(e.at[j, 1], e.at[j, 1], j, 2, dev_x(1))).wait_recv()
        d[j, xm, 32:64] = (d[j, xm, 32:64].astype(F32) + e[j, 1].astype(F32)).astype(BF16)
        send(*ring(d.at[j, xm], f.at[j, 1], j, 4, dev_x(-1)))

    def finish(j):
        remote(*ring(f.at[j, 0], f.at[j, 0], j, 3, dev_x(-1))).wait_recv()
        remote(*ring(f.at[j, 1], f.at[j, 1], j, 4, dev_x(1))).wait_recv()
        total = d[j, x].astype(F32) + f[j, 0].astype(F32) + f[j, 1].astype(F32)
        n = (z + order[j]) % NZ
        out_ref[:, pl.ds(pl.multiple_of(n * SLAB, SLAB), SLAB)] = total.astype(BF16)

    def run(steps):
        for stage, j in steps:
            (project, pair, relay, finish)[stage](j)

    run(((0, 0), (0, 1), (0, 2), (1, 0), (1, 1)))
    o0.second(3)
    run(((0, 3), (0, 4), (1, 2), (2, 0), (2, 1), (1, 3), (1, 4)))
    o0.second(4)
    run(((2, 2), (2, 3), (3, 0), (3, 1)))
    o0.second(5)
    run(((0, 5), (0, 6), (2, 4), (3, 2), (1, 5), (1, 6)))
    o0.second(6)
    run(((0, 7), (3, 3), (2, 5), (2, 6), (1, 7), (3, 4), (3, 5), (3, 6), (2, 7), (3, 7)))
    for copy in sent:
        copy.wait_send()
    lax.fori_loop(1, 64, end_tile, 0)


def shards(normed, qkv_weight, out_weight, segment_ids):
    rows = normed.reshape(PATCHES, WIDTH)
    tiles = normed.reshape(NZ, NY, 8, WIDTH)
    dma = pltpu.SemaphoreType.DMA
    out = pl.pallas_call(
        kernel,
        out_shape=jax.ShapeDtypeStruct((64, WIDTH), BF16),
        in_specs=[pl.BlockSpec(memory_space=pltpu.SMEM)] + [pl.BlockSpec(memory_space=pl.ANY)] * 4,
        out_specs=pl.BlockSpec(memory_space=pltpu.VMEM),
        scratch_shapes=[
            pltpu.VMEM((PATCHES, WIDTH), BF16),
            pltpu.VMEM((PATCHES, WIDTH), BF16),
            pltpu.VMEM((2, NZ, NY, PIECE, 2 * QKV), BF16),
            pltpu.VMEM((NZ, NY, PIECE, 4 * HEAD), BF16),
            pltpu.VMEM((NZ, NY, 8, SLAB), BF16),
            pltpu.VMEM((8, NZ, NY, 8, SLAB), BF16),
            pltpu.VMEM((PATCHES, 2 * QKV), F32),
            pltpu.VMEM((PATCHES, 2 * QKV), BF16),
            pltpu.VMEM((PATCHES, 2 * QKV), BF16),
            pltpu.VMEM((NZ, NY, 8, 2 * HEAD), BF16),
            pltpu.VMEM((NZ, NY, 8, 2 * HEAD), BF16),
            pltpu.VMEM((NZ, NY, 8, 2 * HEAD), BF16),
            pltpu.VMEM((PATCHES, 4 * HEAD), BF16),
            pltpu.VMEM((8, NX, 2, 64, SLAB), BF16),
            pltpu.VMEM((8, NX, 64, SLAB), BF16),
            pltpu.VMEM((8, NX, 64, SLAB), BF16),
            pltpu.VMEM((8, 2, 32, SLAB), BF16),
            pltpu.VMEM((8, 2, 64, SLAB), BF16),
            pltpu.VMEM((PATCHES, HEAD), jnp.int32),
            pltpu.VMEM((8, PATCHES), jnp.int32),
            pltpu.VMEM((PIECE, 4, QKV), BF16),
            dma((6, 21)), dma((6, 21)),
            dma((63,)), dma((63,)),
            dma((8,)), dma((8,)),
            dma((14,)), dma((14,)),
            dma((8, 5)), dma((8, 5)),
            dma((8,)),
        ],
        compiler_params=pltpu.CompilerParams(
            collective_id=0, has_side_effects=True, vmem_limit_bytes=60 * 2**20
        ),
        name="whole",
    )(segment_ids, rows, tiles, qkv_weight, out_weight)
    return out.reshape(1, 64, WIDTH)


def solution(mesh):
    return jax.shard_map(
        shards,
        mesh=mesh,
        in_specs=(P("fsdp", None, None), P("fsdp", "st", None), P("fsdp", "st"), P()),
        out_specs=P("fsdp", "st", None),
        check_vma=False,
    )
```

```python
import functools
import math

import jax
import jax.numpy as jnp
from jax import lax
from jax.experimental import pallas as pl
from jax.experimental.pallas import tpu as pltpu
from jax.sharding import PartitionSpec as P

HEAD = 128
MESH = pl.DeviceIdType.MESH
NZ = NY = 8
NX = 4
PIECE = 48
QKV = 3 * HEAD
SLAB = 384
PATCHES = 512
WIDTH = 3072
UP = ((-1, 0), (-1, 1), (-2, 0), (-2, 1), (-3, 0), (-3, 1), (-4, 0))
DOWN = ((1, 1), (1, 0), (2, 1), (2, 0), (3, 1), (3, 0), (4, 1))
SPREAD = (1, 7, 2, 6, 3, 5, 4)
F32 = jnp.float32
BF16 = jnp.bfloat16


def nt_dot(a, b):
    return lax.dot_general(a, b, (((1,), (1,)), ((), ())), preferred_element_type=F32)


def nn_dot(a, b):
    return lax.dot_general(a, b, (((1,), (0,)), ((), ())), preferred_element_type=F32)


def softmax_rows(scores):
    top = jnp.max(scores, axis=-1, keepdims=True)
    expo = jnp.exp(scores - top)
    return expo * (1.0 / jnp.sum(expo, axis=-1, keepdims=True))


def kernel(
    seg_ref, x_ref, x4_ref, wq_ref, wo_ref, out_ref,
    xs, xt, w, wo, stage, a, acc, qt, qs, ot, b1, b2, ho, p, c, d, e, f, idc, idr, raw,
    gs, gr, ns, nr, xsem, xrec, ts, tr, vs, vr, loc,
):
    st, fs = lax.axis_index("st"), lax.axis_index("fsdp")
    x, core = st // 2, st % 2
    z, y = fs // NY, fs % NY
    scale = 1.0 / math.sqrt(HEAD)
    sent = []

    def dev_y(k):
        return (st, z * NY + (y + k) % NY)

    def dev_z(k):
        return (st, ((z + k) % NZ) * NY + y)

    def dev_x(k):
        return (((x + k) % NX) * 2 + core, fs)

    sibling = (x * 2 + 1 - core, fs)

    def remote(src, dst, ssem, rsem, dev):
        return pltpu.make_async_remote_copy(
            src_ref=src, dst_ref=dst, send_sem=ssem, recv_sem=rsem, device_id=dev, device_id_type=MESH
        )

    def send(*args):
        copy = remote(*args)
        copy.start()
        sent.append(copy)

    barrier = pltpu.get_barrier_semaphore()

    def greet(k, _):
        pl.semaphore_signal(barrier, inc=1, device_id=(st, (fs + k) % 64), device_id_type=MESH)
        return 0

    lax.fori_loop(1, 64, greet, 0)
    for dev in (dev_x(1), dev_x(-1), sibling):
        pl.semaphore_signal(barrier, inc=1, device_id=dev, device_id_type=MESH)

    cols = pl.ds(pl.multiple_of(st * SLAB, SLAB), SLAB)
    locals_ = [
        pltpu.make_async_copy(x4_ref.at[:, :, :, cols], stage, loc.at[0]),
        pltpu.make_async_copy(wo_ref, wo.at[z, y], loc.at[1]),
        pltpu.make_async_copy(wq_ref, raw, loc.at[2]),
        pltpu.make_async_copy(x_ref, xs, loc.at[4]),
    ]
    for cp in locals_:
        cp.start()

    sub8 = lax.broadcasted_iota(jnp.int32, (8, HEAD), 0)
    lane = lax.broadcasted_iota(jnp.int32, (8, PATCHES), 1)
    row = jnp.zeros((8, PATCHES), jnp.int32)
    for t in range(64):
        sid = seg_ref[t]
        idc[t * 8 : (t + 1) * 8, :] = sub8 + sid * 8
        row = jnp.where(lane // 8 == t, sid * 8, row)
    idr[...] = row + lane % 8

    for cp in locals_[:3]:
        cp.wait()
    for h in range(4):
        w[h // 2, z, y, :, h % 2 * QKV : (h % 2 + 1) * QKV] = raw[:, h, :]
    own_tile = pltpu.make_async_copy(stage.at[z, y], a.at[st, z, y], loc.at[5])
    own_tile.start()
    own_tile.wait()
    pl.semaphore_wait(barrier, 66)

    class Stream:
        def __init__(self, number, y_first, flip, view):
            self.n, self.y_first, self.flip, self.view = number, y_first, flip, view
            self.ac, self.bc = (y, z) if y_first else (z, y)
            self.da, self.db = (dev_y, dev_z) if y_first else (dev_z, dev_y)

        def piece(self, at):
            return self.view(self.bc, at) if self.y_first else self.view(at, self.bc)

        def slab(self, bt, sub):
            four = pl.ds(4 * sub, 4)
            return self.view(bt, four) if self.y_first else self.view(four, bt)

        def sems(self, i):
            return gs.at[self.n, i], gr.at[self.n, i]

        def first_own(self):
            right = 1 if not self.flip else -1
            own = self.piece(self.ac)
            send(own, own, *self.sems(0), self.da(right))
            send(own, own, *self.sems(4), self.da(-right))

        def first(self, k):
            right = 1 if not self.flip else -1
            for way, base, last in ((right, 0, 4), (-right, 4, 3)):
                if k <= last:
                    got = self.piece((self.ac - way * k) % 8)
                    remote(got, got, *self.sems(base + k - 1), self.da(-way)).wait_recv()
                    if k < last:
                        send(got, got, *self.sems(base + k), self.da(way))

        def second_own(self):
            for sub in (0, 1):
                for way, base, chain in ((1, 7, UP), (-1, 14, DOWN)):
                    blk = self.slab(self.bc, chain[sub][1])
                    send(blk, blk, *self.sems(base + sub), self.db(way))

        def second(self, i):
            for way, base, chain in ((1, 7, UP), (-1, 14, DOWN)):
                off, sub = chain[i]
                got = self.slab((self.bc + off) % 8, sub)
                remote(got, got, *self.sems(base + i), self.db(-way)).wait_recv()
                if i <= 4:
                    send(got, got, *self.sems(base + i + 2), self.db(way))

    def head_stream(number, kind, h, y_first, flip):
        return Stream(number, y_first, flip, lambda zi, yi: w.at[kind, zi, yi, ..., pl.ds(h * QKV, QKV)])

    t0 = head_stream(0, 1, 0, True, False)
    t1 = head_stream(1, 1, 1, False, True)
    s0 = head_stream(2, 0, 0, True, True)
    s1 = head_stream(3, 0, 1, False, False)
    o0 = Stream(4, True, False, lambda zi, yi: wo.at[zi, yi, ..., pl.ds(0, 32), :])
    o1 = Stream(5, False, True, lambda zi, yi: wo.at[zi, yi, ..., pl.ds(32, 16), :])

    def both(one, two, i):
        one.second(i)
        two.second(i)

    t0.first_own()
    t1.first_own()

    def tile_out(k):
        to = (fs + 27 * k) % 64
        return remote(stage.at[to // NY, to % NY], a.at[st, z, y], ns.at[k - 1], nr.at[k - 1], (st, to))

    def tile_in(k):
        to = (fs + 37 * k) % 64
        got = a.at[st, to // NY, to % NY]
        return remote(got, got, ns.at[k - 1], nr.at[k - 1], (st, to))

    def start_tile(k, _):
        tile_out(k).start()
        return 0

    def await_tile(k, _):
        tile_in(k).wait_recv()
        return 0

    def end_tile(k, _):
        tile_out(k).wait_send()
        return 0

    others = (s0, s1, o1, o0)
    for s in others:
        s.first_own()
    for k in range(1, 5):
        lax.fori_loop(16 * k - 15, min(16 * k + 1, 64), start_tile, 0)
        t0.first(k)
        t1.first(k)
    t0.second_own()
    t1.second_own()

    def first_others(k):
        for s in others:
            s.first(k)

    first_others(1)
    first_others(2)

    def assemble(sl):
        def body(i, _):
            v = a[sl, i].astype(F32).reshape(64, SLAB).astype(BF16)
            rows = pl.ds(pl.multiple_of(i * 64, 64), 64)
            xt[rows, pl.ds(pl.multiple_of(sl * SLAB, SLAB), SLAB)] = v
            return 0

        lax.fori_loop(0, 8, body, 0)

    sl_m, sl_p, sl_2 = (((x + k) % NX) * 2 + core for k in (3, 1, 2))
    lo, hi = pl.ds(0, 4), pl.ds(4, 4)

    def xmove(ref, i, dev):
        return ref, ref, xsem.at[i], xrec.at[i], dev

    def from_sibling(i, sl):
        other = sl + 1 - 2 * core
        remote(*xmove(a.at[other], 4 + i, sibling)).wait_recv()
        assemble(other)

    lax.fori_loop(1, 64, await_tile, 0)
    send(*xmove(a.at[st], 0, dev_x(1)))
    send(*xmove(a.at[st], 1, dev_x(-1)))
    send(*xmove(a.at[st], 4, sibling))
    both(t0, t1, 0)
    first_others(3)
    assemble(st)
    both(t0, t1, 1)
    first_others(4)
    from_sibling(0, st)
    both(t0, t1, 2)
    remote(*xmove(a.at[sl_m], 0, dev_x(-1))).wait_recv()
    send(*xmove(a.at[sl_m, lo], 2, dev_x(1)))
    send(*xmove(a.at[sl_m], 5, sibling))
    remote(*xmove(a.at[sl_p], 1, dev_x(1))).wait_recv()
    send(*xmove(a.at[sl_p, hi], 3, dev_x(-1)))
    send(*xmove(a.at[sl_p], 6, sibling))
    assemble(sl_m)
    both(t0, t1, 3)
    assemble(sl_p)
    both(t0, t1, 4)
    s0.second_own()
    s1.second_own()
    remote(*xmove(a.at[sl_2, lo], 2, dev_x(-1))).wait_recv()
    remote(*xmove(a.at[sl_2, hi], 3, dev_x(1))).wait_recv()
    send(*xmove(a.at[sl_2], 7, sibling))
    assemble(sl_2)
    from_sibling(1, sl_m)
    both(t0, t1, 5)
    from_sibling(2, sl_p)
    from_sibling(3, sl_2)
    both(t0, t1, 6)

    def proj(rows, kind, i):
        part = nn_dot(rows[:, i * 2 * SLAB : (i + 1) * 2 * SLAB], w[kind, 2 * i : 2 * i + 2].reshape(2 * SLAB, 2 * QKV))
        acc[...] = part if i == 0 else acc[...] + part

    def proj_slab(off, first=False):
        n = (z + off) % NZ
        part = nn_dot(
            xs[:, pl.ds(pl.multiple_of(n * SLAB, SLAB), SLAB)], w[0, n, :, :, 0:QKV].reshape(SLAB, QKV)
        )
        acc[:, 0:QKV] = part if first else acc[:, 0:QKV] + part

    def proj_second(i):
        part = nn_dot(
            xs[:, i * 2 * SLAB : (i + 1) * 2 * SLAB],
            w[0, 2 * i : 2 * i + 2, :, :, QKV:].reshape(2 * SLAB, QKV),
        )
        acc[:, QKV:] = part if i == 0 else acc[:, QKV:] + part

    def temporal(h):
        base = h * QKV
        for b, start in enumerate((0, 64, 192, 256)):
            rows, keys = pl.ds(b * 128, 128), pl.ds(start, 256)
            s = nt_dot(qt[rows, base : base + HEAD], qt[keys, base + HEAD : base + 2 * HEAD]) * scale
            same = idc[rows, 0:1] == idr[0:1, keys]
            wt = softmax_rows(jnp.where(same, s, -1e30)).astype(BF16)
            o = nn_dot(wt, qt[keys, base + 2 * HEAD : base + QKV])
            ot[2 * b : 2 * b + 2, :, :, h * HEAD : (h + 1) * HEAD] = o.reshape(2, 8, 8, HEAD).astype(BF16)

    def spatial(h, half):
        base = h * QKV
        rows = pl.ds(half * 256, 256)
        s = nt_dot(qs[rows, base : base + HEAD], qs[:, base + HEAD : base + 2 * HEAD]) * scale
        o = nn_dot(softmax_rows(s).astype(BF16), qs[:, base + 2 * HEAD : base + QKV])
        ho[rows, h * HEAD : (h + 1) * HEAD] = o.astype(BF16)

    proj(xt, 1, 0)
    both(s0, s1, 0)
    proj(xt, 1, 1)
    proj(xt, 1, 2)
    proj(xt, 1, 3)
    qt[...] = acc[...].astype(BF16)
    both(s0, s1, 1)
    temporal(0)
    temporal(1)
    for k in SPREAD:
        send(ot.at[(z + k) % NZ], b1.at[z], ts.at[k - 1], tr.at[k - 1], dev_z(k))
    back = pltpu.make_async_copy(ot.at[z], b1.at[z], loc.at[6])
    back.start()
    locals_[3].wait()
    both(s0, s1, 2)
    proj_slab(0, True)
    back.wait()
    for k in range(1, 8):
        got = b1.at[(z - k) % NZ]
        remote(got, got, ts.at[k - 1], tr.at[k - 1], dev_z(-k)).wait_recv()
    for k in SPREAD:
        send(b1.at[:, (y + k) % NY], b2.at[:, y], ts.at[6 + k], tr.at[6 + k], dev_y(k))
    back2 = pltpu.make_async_copy(b1.at[:, y], b2.at[:, y], loc.at[7])
    back2.start()
    both(s0, s1, 3)
    both(s0, s1, 4)
    o1.second_own()
    o0.second_own()
    proj_slab(-1)
    proj_slab(1)
    both(s0, s1, 5)
    proj_slab(-2)
    proj_slab(2)
    o1.second(0)
    both(s0, s1, 6)
    o1.second(1)
    o0.second(0)
    proj_slab(-3)
    proj_slab(3)
    o1.second(2)
    proj_slab(4)
    o1.second(3)
    o0.second(1)
    proj_second(0)
    proj_second(1)
    o1.second(4)
    proj_second(2)
    proj_second(3)
    qs[...] = acc[...].astype(BF16)
    o1.second(5)
    o0.second(2)
    spatial(0, 0)
    spatial(0, 1)
    o1.second(6)
    back2.wait()
    for k in range(1, 8):
        got = b2.at[:, (y - k) % NY]
        remote(got, got, ts.at[6 + k], tr.at[6 + k], dev_y(-k)).wait_recv()
    for i in range(8):
        ho[i * 64 : (i + 1) * 64, 2 * HEAD :] = b2[i].astype(F32).reshape(64, 2 * HEAD).astype(BF16)
    o0.second(3)
    spatial(1, 0)
    spatial(1, 1)

    order = (0, -1, 1, -2, 2, -3, 3, 4)
    xp, xm, x2 = (x + 1) % NX, (x + 3) % NX, (x + 2) % NX
    top, low = pl.ds(0, 32), pl.ds(32, 32)

    def ring(ref_from, ref_to, j, i, dev):
        return ref_from, ref_to, vs.at[j, i], vr.at[j, i], dev

    def project(j):
        n = (z + order[j]) % NZ
        o = nt_dot(ho[...], wo[n].reshape(SLAB, 4 * HEAD))
        p[j] = o.astype(BF16).reshape(NX, 2, 64, SLAB)
        send(*ring(p.at[j, :, 1 - core], c.at[j], j, 0, sibling))

    def pair(j):
        remote(*ring(c.at[j], c.at[j], j, 0, sibling)).wait_recv()
        d[j] = (p[j, :, core].astype(F32) + c[j].astype(F32)).astype(BF16)
        send(*ring(d.at[j, x2, top], e.at[j, 0], j, 1, dev_x(1)))
        send(*ring(d.at[j, x2, low], e.at[j, 1], j, 2, dev_x(-1)))

    def relay(j):
        remote(*ring(e.at[j, 0], e.at[j, 0], j, 1, dev_x(-1))).wait_recv()
        d[j, xp, 0:32] = (d[j, xp, 0:32].astype(F32) + e[j, 0].astype(F32)).astype(BF16)
        send(*ring(d.at[j, xp], f.at[j, 0], j, 3, dev_x(1)))
        remote(*ring(e.at[j, 1], e.at[j, 1], j, 2, dev_x(1))).wait_recv()
        d[j, xm, 32:64] = (d[j, xm, 32:64].astype(F32) + e[j, 1].astype(F32)).astype(BF16)
        send(*ring(d.at[j, xm], f.at[j, 1], j, 4, dev_x(-1)))

    def finish(j):
        remote(*ring(f.at[j, 0], f.at[j, 0], j, 3, dev_x(-1))).wait_recv()
        remote(*ring(f.at[j, 1], f.at[j, 1], j, 4, dev_x(1))).wait_recv()
        total = d[j, x].astype(F32) + f[j, 0].astype(F32) + f[j, 1].astype(F32)
        n = (z + order[j]) % NZ
        out_ref[:, pl.ds(pl.multiple_of(n * SLAB, SLAB), SLAB)] = total.astype(BF16)

    for j in range(14):
        if j in (1, 4, 6):
            o0.second({1: 4, 4: 5, 6: 6}[j])
        if j < 8:
            project(j)
        if 2 <= j <= 9:
            pair(j - 2)
        if 4 <= j <= 11:
            relay(j - 4)
        if 6 <= j:
            finish(j - 6)
    for copy in sent:
        copy.wait_send()
    lax.fori_loop(1, 64, end_tile, 0)


def shards(normed, qkv_weight, out_weight, segment_ids):
    rows = normed.reshape(PATCHES, WIDTH)
    tiles = normed.reshape(NZ, NY, 8, WIDTH)
    dma = pltpu.SemaphoreType.DMA
    out = pl.pallas_call(
        kernel,
        out_shape=jax.ShapeDtypeStruct((64, WIDTH), BF16),
        in_specs=[pl.BlockSpec(memory_space=pltpu.SMEM)] + [pl.BlockSpec(memory_space=pl.ANY)] * 4,
        out_specs=pl.BlockSpec(memory_space=pltpu.VMEM),
        scratch_shapes=[
            pltpu.VMEM((PATCHES, WIDTH), BF16),
            pltpu.VMEM((PATCHES, WIDTH), BF16),
            pltpu.VMEM((2, NZ, NY, PIECE, 2 * QKV), BF16),
            pltpu.VMEM((NZ, NY, PIECE, 4 * HEAD), BF16),
            pltpu.VMEM((NZ, NY, 8, SLAB), BF16),
            pltpu.VMEM((8, NZ, NY, 8, SLAB), BF16),
            pltpu.VMEM((PATCHES, 2 * QKV), F32),
            pltpu.VMEM((PATCHES, 2 * QKV), BF16),
            pltpu.VMEM((PATCHES, 2 * QKV), BF16),
            pltpu.VMEM((NZ, NY, 8, 2 * HEAD), BF16),
            pltpu.VMEM((NZ, NY, 8, 2 * HEAD), BF16),
            pltpu.VMEM((NZ, NY, 8, 2 * HEAD), BF16),
            pltpu.VMEM((PATCHES, 4 * HEAD), BF16),
            pltpu.VMEM((8, NX, 2, 64, SLAB), BF16),
            pltpu.VMEM((8, NX, 64, SLAB), BF16),
            pltpu.VMEM((8, NX, 64, SLAB), BF16),
            pltpu.VMEM((8, 2, 32, SLAB), BF16),
            pltpu.VMEM((8, 2, 64, SLAB), BF16),
            pltpu.VMEM((PATCHES, HEAD), jnp.int32),
            pltpu.VMEM((8, PATCHES), jnp.int32),
            pltpu.VMEM((PIECE, 4, QKV), BF16),
            dma((6, 21)), dma((6, 21)),
            dma((63,)), dma((63,)),
            dma((8,)), dma((8,)),
            dma((14,)), dma((14,)),
            dma((8, 5)), dma((8, 5)),
            dma((8,)),
        ],
        compiler_params=pltpu.CompilerParams(
            collective_id=0, has_side_effects=True, vmem_limit_bytes=60 * 2**20
        ),
        name="whole",
    )(segment_ids, rows, tiles, qkv_weight, out_weight)
    return out.reshape(1, 64, WIDTH)


def solution(mesh):
    return jax.shard_map(
        shards,
        mesh=mesh,
        in_specs=(P("fsdp", None, None), P("fsdp", "st", None), P("fsdp", "st"), P()),
        out_specs=P("fsdp", "st", None),
        check_vma=False,
    )
```
